32 devices in a mesh: dp: 8 (over z, y), seq: 4 (over x, core).
Axes of the slice: x: 2, y: 2, z: 4, core: 2. Of those that a mesh axis runs over, the one named last changes fastest.
Arguments:
- tokens: float32 [16, 2048, 768], P('dp', 'seq'), may hold values from -6 to 6
- timesteps: int32 [16], P('dp'), may hold values from 0 to 1999
- lengths: int32 [16], P('dp'), may hold values from 512 to 2048, as said below
- time_weight: float32 [768, 768], P('dp'), may hold values from -0.21875 to 0.21875
- attn_gain: float32 [768], P('dp'), may hold values from 0.5 to 1.5
- attn_shift: float32 [768], P('dp'), may hold values from -4 to 4
- qkv_weight: float32 [768, 2304], P('dp'), may hold values from -0.21875 to 0.21875
- out_weight: float32 [768, 768], P('dp'), may hold values from -6 to 6
- out_bias: float32 [768], P('dp'), may hold values from -4 to 4
- mlp_gain: float32 [768], P('dp'), may hold values from 0.5 to 1.5
- mlp_shift: float32 [768], P('dp'), may hold values from -4 to 4
- up_weight: float32 [768, 3072], P('dp'), may hold values from -0.21875 to 0.21875
- up_bias: float32 [3072], P('dp'), may hold values from -6 to 6
- down_weight: float32 [3072, 768], P('dp'), may hold values from -0.109375 to 0.109375
- down_bias: float32 [768], P('dp'), may hold values from -4 to 4
- cotangent: float32 [16, 2048, 768], P('dp', 'seq'), may hold values from -6 to 6
Outputs:
- result: float32 [16, 2048, 768], P('dp', 'seq')
- tokens_grad: float32 [16, 2048, 768], P('dp', 'seq')
- time_weight_grad: float32 [768, 768], P('dp')
- attn_gain_grad: float32 [768], P('dp')
- attn_shift_grad: float32 [768], P('dp')
- qkv_weight_grad: float32 [768, 2304], P('dp')
- out_weight_grad: float32 [768, 768], P('dp')
- out_bias_grad: float32 [768], P('dp')
- mlp_gain_grad: float32 [768], P('dp')
- mlp_shift_grad: float32 [768], P('dp')
- up_weight_grad: float32 [768, 3072], P('dp')
- up_bias_grad: float32 [3072], P('dp')
- down_weight_grad: float32 [3072, 768], P('dp')
- down_bias_grad: float32 [768], P('dp')
The draws below stay inside these ranges and needn't reach their ends.
Inputs may be any that keep to these rules, and one draw needn't show every extreme that they name: Slots of sequence s at positions below lengths[s] hold tokens, the others are padding; some sequence is full and some has 512 used slots.
All inputs are finite; a program needn't handle non-finite values.
Results may differ from the reference program's by a relative error of at most 0.013.
Values may be sent and summed in bfloat16 or wider, within the bound.
No kernel may reach another device: no remote copies, remote signals or barrier semaphores. Data moves between devices by JAX's collectives and lax.ppermute only.
A program may use at most 192 MiB of HBM per device.

```python
import math
import jax
import jax.numpy as jnp
from jax import lax

D = 768
H = 12
HEAD = 64
FF = 3072
LENGTH = 2048
SEQUENCES = 16


def draw_lengths(key, part):
    first, second, third = jax.random.split(key, 3)
    values = jax.random.randint(first, (SEQUENCES,), LENGTH // 4, LENGTH + 1)
    spot_full = jax.random.randint(second, (), 0, SEQUENCES)
    spot_short = (spot_full + 1 + jax.random.randint(third, (), 0, SEQUENCES - 1)) % SEQUENCES
    order = jnp.arange(SEQUENCES)
    values = jnp.where(order == spot_full, LENGTH, values)
    values = jnp.where(order == spot_short, LENGTH // 4, values)
    return values.astype(jnp.int32)


def with_ends(result, own_key, smallest, largest):
    place = [jax.random.randint(jax.random.fold_in(own_key, axis), (), 0, length) for axis, length in enumerate(result.shape)]
    longest = result.shape.index(max(result.shape))
    beside = place[:longest] + [(place[longest] + 1) % result.shape[longest]] + place[longest + 1:]
    return result.at[tuple(place)].set(smallest).at[tuple(beside)].set(largest)


def steps_of(key, shape, shards, least, high):
    level = 1.0
    for axis_at, blocks in shards:
        steps = jax.random.uniform(jax.random.fold_in(jax.random.fold_in(key, 6), axis_at), (blocks,), jnp.float32, least / len(shards), high / len(shards))
        level = level * jnp.repeat(jnp.exp(steps), shape[axis_at] // blocks).reshape((-1,) + (1,) * (len(shape) - 1 - axis_at))
    return level


def normal_values(rng, dims, scale, reach, shards=(), held_as=jnp.bfloat16):
    values = jax.random.normal(rng, dims, jnp.float32) * scale
    if len(shards) > 0:
        values = steps_of(rng, dims, shards, -0.22, 0.18) * values
    return jnp.clip(values, min=-reach, max=reach).astype(held_as)


def setup_inputs(seed: int = 0) -> dict:
    arg_keys = jax.random.split(jax.random.key(seed), 17)
    tokens = normal_values(arg_keys[0], (SEQUENCES, LENGTH, D), 1.0, 6.0, ((0, 8), (1, 4)), jnp.float32)
    timesteps = with_ends(jax.random.randint(arg_keys[1], (SEQUENCES,), 0, 2000), jax.random.fold_in(arg_keys[1], 1), 0, 1999).astype(jnp.int32)
    lengths = draw_lengths(jax.random.fold_in(arg_keys[16], 71), 0)
    time_weight = normal_values(arg_keys[3], (D, D), D ** -0.5, 0.21875, ((0, 8),), jnp.float32)
    attn_gain = jnp.clip(1.0 + 0.1 * jax.random.normal(arg_keys[4], (D,), jnp.float32), 0.5, 1.5)
    attn_shift = normal_values(arg_keys[5], (D,), 0.3, 4.0, ((0, 8),), jnp.float32)
    qkv_weight = normal_values(arg_keys[6], (D, 3 * D), D ** -0.5, 0.21875, ((0, 8),), jnp.float32)
    out_weight = normal_values(arg_keys[7], (D, D), (max(1, 2 * D // LENGTH)) ** -0.5, 6.0, ((0, 8),), jnp.float32)
    out_bias = normal_values(arg_keys[8], (D,), 0.3, 4.0, ((0, 8),), jnp.float32)
    mlp_gain = jnp.clip(1.0 + 0.1 * jax.random.normal(arg_keys[9], (D,), jnp.float32), 0.5, 1.5)
    mlp_shift = normal_values(arg_keys[10], (D,), 0.3, 4.0, ((0, 8),), jnp.float32)
    up_weight = normal_values(arg_keys[11], (D, FF), D ** -0.5, 0.21875, ((0, 8),), jnp.float32)
    up_bias = normal_values(arg_keys[12], (FF,), 0.5, 6.0, ((0, 8),), jnp.float32)
    down_weight = normal_values(arg_keys[13], (FF, D), FF ** -0.5, 0.109375, ((0, 8),), jnp.float32)
    down_bias = normal_values(arg_keys[14], (D,), 0.3, 4.0, ((0, 8),), jnp.float32)
    cotangent = normal_values(arg_keys[15], (SEQUENCES, LENGTH, D), 1.0, 6.0, ((0, 8), (1, 4)), jnp.float32)
    return dict(tokens=tokens, timesteps=timesteps, lengths=lengths, time_weight=time_weight, attn_gain=attn_gain, attn_shift=attn_shift, qkv_weight=qkv_weight, out_weight=out_weight, out_bias=out_bias, mlp_gain=mlp_gain, mlp_shift=mlp_shift, up_weight=up_weight, up_bias=up_bias, down_weight=down_weight, down_bias=down_bias, cotangent=cotangent)


@jax.custom_vjp
def low(v):
    return lax.optimization_barrier(v.astype(jnp.bfloat16)).astype(jnp.float32)

@jax.custom_vjp
def low_back(v):
    return v

def low_keep(v):
    return (low(v), None)

def low_pass(kept, grad):
    return (grad,)

def back_keep(v):
    return (v, None)

def back_low(kept, grad):
    return (low(grad),)
low.defvjp(low_keep, low_pass)
low_back.defvjp(back_keep, back_low)
epsilon = 1e-05

def sinusoid(steps_given):
    half = D // 2
    freqs = jnp.exp(-math.log(10000.0) * jnp.arange(half, dtype=jnp.float32) / half)
    angles = steps_given.astype(jnp.float32)[..., None] * freqs
    return jnp.concatenate([jnp.sin(angles), jnp.cos(angles)], axis=-1)

def normalize(values, gain, shift):
    center = values - lax.optimization_barrier(jnp.mean(values, axis=-1, keepdims=True))
    spread = lax.optimization_barrier(jnp.mean(center * center, axis=-1, keepdims=True))
    return center * lax.rsqrt(spread + epsilon) * gain + shift

def product(left, right):
    return jnp.dot(left, right, precision=lax.Precision.HIGHEST)

def attention(queries, keys, values, valid):
    block = min(512, LENGTH)
    count = LENGTH // block
    scale = 1.0 / math.sqrt(HEAD)
    key_heads = keys.reshape(LENGTH, H, HEAD)
    value_heads = values.reshape(LENGTH, H, HEAD)

    def one_block(query_block):
        scores = low_back(scale * jnp.einsum('qhd,khd->hqk', query_block, key_heads, precision=lax.Precision.HIGHEST))
        scores = jnp.where(valid, scores, -1e+30)
        probs = low(jax.nn.softmax(scores, axis=-1))
        return jnp.einsum('hqk,khd->qhd', probs, value_heads, precision=lax.Precision.HIGHEST)
    mixed = lax.map(jax.checkpoint(one_block), queries.reshape(count, block, H, HEAD))
    return mixed.reshape(LENGTH, D)

def layer(weights, values, emb_row, valid):
    rounded = [low(item) for item in weights]
    time_w, gain_a, shift_a, qkv_w, out_w, out_b, gain_m, shift_m, up_w, up_b, down_w, down_b = rounded
    hidden = values + product(low(emb_row)[None, :], time_w)
    normed_one = low(normalize(hidden, gain_a, shift_a))
    projected = product(normed_one, qkv_w)
    queries = low(low_back(projected[:, :D]))
    keys = low(low_back(projected[:, D:2 * D]))
    vals = low(low_back(projected[:, 2 * D:]))
    mixed = low(low_back(attention(queries, keys, vals, valid)))
    middle = hidden + low_back(product(mixed, out_w) + out_b)
    normed_two = low(normalize(middle, gain_m, shift_m))
    pre_act = low_back(product(normed_two, up_w) + up_b)
    activated = low(jax.nn.gelu(pre_act, approximate=False))
    return jnp.where(valid[:, None], middle + low_back(product(activated, down_w) + down_b), 0.0)

def reference(tokens, timesteps, lengths, time_weight, attn_gain, attn_shift, qkv_weight, out_weight, out_bias, mlp_gain, mlp_shift, up_weight, up_bias, down_weight, down_bias, cotangent):
    params = (time_weight, attn_gain, attn_shift, qkv_weight, out_weight, out_bias, mlp_gain, mlp_shift, up_weight, up_bias, down_weight, down_bias)
    embedded = sinusoid(timesteps)
    positions = jnp.arange(LENGTH, dtype=jnp.int32)

    def one_sequence(totals, items):
        source, emb_row, length, grad_row = items
        valid = positions < length.astype(jnp.int32)

        def forward(weights, values):
            return layer(weights, values, emb_row, valid)
        output, pull = jax.vjp(forward, params, source)
        grad_weights, grad_tokens = pull(grad_row)
        totals = jax.tree.map(lambda left, right: left + right, totals, grad_weights)
        return (totals, (output, grad_tokens))
    zeros = jax.tree.map(jnp.zeros_like, params)
    totals, (outputs, grads) = lax.scan(one_sequence, zeros, (tokens, embedded, lengths, cotangent))
    return (outputs, grads, totals[0], totals[1], totals[2], totals[3], totals[4], totals[5], totals[6], totals[7], totals[8], totals[9], totals[10], totals[11])
```

```python
import functools, math
import jax, jax.numpy as jnp
from jax import lax
from jax.experimental import pallas as pl
from jax.experimental.pallas import tpu as pltpu
from jax.sharding import PartitionSpec as P

HEAD = 64
PAIR = 2 * HEAD
NT = (((1,), (1,)), ((), ()))
NN = (((1,), (0,)), ((), ()))
SCALE = 1.0 / math.sqrt(HEAD)


def dot32(left, right, dims):
    return lax.dot_general(left, right, dims, preferred_element_type=jnp.float32)


def one_head(block, which):
    lane = lax.broadcasted_iota(jnp.int32, block.shape, 1)
    return jnp.where(lane // HEAD == which, block.astype(jnp.float32), 0.0)


def attention_forward_kernel(bias_ref, q_ref, k_ref, v_ref, out_ref, log_ref, vt_ref, *, chunk):
    @pl.when(pl.program_id(1) == 0)
    def _():
        vt_ref[...] = v_ref[...].T

    total = k_ref.shape[0]
    mixed = []
    for which in range(2):
        query = (one_head(q_ref[...], which) * SCALE).astype(jnp.bfloat16)
        scores = []
        for start in range(0, total, chunk):
            rows = pl.ds(start, chunk)
            part = dot32(k_ref[rows, :], query, NT) + bias_ref[rows, :]
            scores.append(part)
        top = jnp.max(scores[0], axis=0, keepdims=True)
        for part in scores[1:]:
            top = jnp.maximum(top, jnp.max(part, axis=0, keepdims=True))
        totals = 0.0
        acc = 0.0
        for index, part in enumerate(scores):
            weights = jnp.exp(part - top)
            totals = totals + jnp.sum(weights, axis=0, keepdims=True)
            values = vt_ref[which * HEAD : (which + 1) * HEAD, index * chunk : (index + 1) * chunk]
            acc = acc + dot32(values, weights.astype(jnp.bfloat16), NN)
        mixed.append(acc / totals)
        log_ref[0, which : which + 1, :] = top + jnp.log(totals)
    out_ref[...] = jnp.concatenate(mixed, axis=0).T.astype(jnp.bfloat16)


def attention_backward_kernel(
    bias_ref, q_ref, k_ref, v_ref, mixed_ref, grad_ref, log_ref,
    dq_ref, dk_ref, dv_ref, kt_ref, dk_acc, dv_acc, *, chunk
):
    step = pl.program_id(1)

    @pl.when(step == 0)
    def _():
        kt_ref[...] = k_ref[...].T
        dk_acc[...] = jnp.zeros_like(dk_acc)
        dv_acc[...] = jnp.zeros_like(dv_acc)

    total = k_ref.shape[0]
    grad32 = grad_ref[...].astype(jnp.float32)
    centre_t = (grad32 * mixed_ref[...].astype(jnp.float32)).T
    queries = []
    grads = []
    for which in range(2):
        queries.append((one_head(q_ref[...], which) * SCALE).astype(jnp.bfloat16))
        grads.append(one_head(grad_ref[...], which).astype(jnp.bfloat16))
    dq_parts = [0.0, 0.0]
    for start in range(0, total, chunk):
        rows = pl.ds(start, chunk)
        dk_part = dk_acc[rows, :]
        dv_part = dv_acc[rows, :]
        for which in range(2):
            head = slice(which * HEAD, (which + 1) * HEAD)
            centre = jnp.sum(centre_t[head, :], axis=0, keepdims=True)
            scores = dot32(k_ref[rows, :], queries[which], NT) + bias_ref[rows, :]
            probs = jnp.exp(scores - log_ref[0, which : which + 1, :])
            grad_probs = dot32(v_ref[rows, :], grads[which], NT)
            grad_scores = (probs * (grad_probs - centre)).astype(jnp.bfloat16)
            dv_part = dv_part + dot32(probs.astype(jnp.bfloat16), grads[which], NN)
            dk_part = dk_part + dot32(grad_scores, queries[which], NN)
            dq_parts[which] = dq_parts[which] + dot32(
                kt_ref[head, start : start + chunk], grad_scores, NN
            )
        dk_acc[rows, :] = dk_part
        dv_acc[rows, :] = dv_part
    dq_ref[...] = (jnp.concatenate(dq_parts, axis=0).T * SCALE).astype(jnp.bfloat16)

    @pl.when(step == pl.num_programs(1) - 1)
    def _():
        dk_ref[...] = dk_acc[...].astype(jnp.bfloat16)
        dv_ref[...] = dv_acc[...].astype(jnp.bfloat16)


def attention_forward(projected, bias, block=512, chunk=512):
    total = projected.shape[0]
    width = projected.shape[1] // 3
    block = min(block, total)
    pairs = width // PAIR
    return pl.pallas_call(
        functools.partial(attention_forward_kernel, chunk=min(chunk, total)),
        name="attention_forward",
        grid=(pairs, total // block),
        in_specs=[
            pl.BlockSpec((total, 1), lambda p, i: (0, 0)),
            pl.BlockSpec((block, PAIR), lambda p, i: (i, p)),
            pl.BlockSpec((total, PAIR), lambda p, i: (0, pairs + p)),
            pl.BlockSpec((total, PAIR), lambda p, i: (0, 2 * pairs + p)),
        ],
        out_specs=[
            pl.BlockSpec((block, PAIR), lambda p, i: (i, p)),
            pl.BlockSpec((1, 2, block), lambda p, i: (p, 0, i)),
        ],
        out_shape=[
            jax.ShapeDtypeStruct((total, width), jnp.bfloat16),
            jax.ShapeDtypeStruct((pairs, 2, total), jnp.float32),
        ],
        scratch_shapes=[pltpu.VMEM((PAIR, total), jnp.bfloat16)],
    )(bias, projected, projected, projected)


def attention_backward(projected, mixed, grad_mixed, logs, bias, block=512, chunk=256):
    total = projected.shape[0]
    width = projected.shape[1] // 3
    block = min(block, total)
    pairs = width // PAIR
    out = jax.ShapeDtypeStruct((total, width), jnp.bfloat16)
    return pl.pallas_call(
        functools.partial(attention_backward_kernel, chunk=min(chunk, total)),
        name="attention_backward",
        grid=(pairs, total // block),
        in_specs=[
            pl.BlockSpec((total, 1), lambda p, i: (0, 0)),
            pl.BlockSpec((block, PAIR), lambda p, i: (i, p)),
            pl.BlockSpec((total, PAIR), lambda p, i: (0, pairs + p)),
            pl.BlockSpec((total, PAIR), lambda p, i: (0, 2 * pairs + p)),
            pl.BlockSpec((block, PAIR), lambda p, i: (i, p)),
            pl.BlockSpec((block, PAIR), lambda p, i: (i, p)),
            pl.BlockSpec((1, 2, block), lambda p, i: (p, 0, i)),
        ],
        out_specs=[
            pl.BlockSpec((block, PAIR), lambda p, i: (i, p)),
            pl.BlockSpec((total, PAIR), lambda p, i: (0, p)),
            pl.BlockSpec((total, PAIR), lambda p, i: (0, p)),
        ],
        out_shape=[out, out, out],
        scratch_shapes=[
            pltpu.VMEM((PAIR, total), jnp.bfloat16),
            pltpu.VMEM((total, PAIR), jnp.float32),
            pltpu.VMEM((total, PAIR), jnp.float32),
        ],
    )(bias, projected, projected, projected, mixed, grad_mixed, logs)


epsilon = 1e-05

CORE_SWAP = ((0, 1), (1, 0), (2, 3), (3, 2))
CHIP_SWAP = ((0, 2), (2, 0), (1, 3), (3, 1))
LOW = jnp.bfloat16
F32 = jnp.float32


def swap_core(values):
    return lax.ppermute(values, "seq", CORE_SWAP)


def swap_chip(values):
    return lax.ppermute(values, "seq", CHIP_SWAP)


def swap_bit(values, size, bit):
    return lax.ppermute(values, "dp", [(i, i ^ bit) for i in range(size)])


def bits_of(size):
    return [1 << b for b in range(size.bit_length() - 1)]


def gather_dp(values, size):
    me = lax.axis_index("dp")
    held = values[None]
    for bit in reversed(bits_of(size)):
        got = swap_bit(held, size, bit)
        upper = (me & bit) != 0
        first = jnp.where(upper, got, held)
        second = jnp.where(upper, held, got)
        held = jnp.stack([first, second], axis=1).reshape((-1,) + values.shape)
    return held


def scatter_dp(values, size, wire):
    me = lax.axis_index("dp")
    held = values
    for bit in bits_of(size):
        upper = (me & bit) != 0
        halves = held.reshape((held.shape[0] // 2, 2) + held.shape[1:])
        send = jnp.where(upper, halves[:, 0], halves[:, 1]).astype(wire)
        keep = jnp.where(upper, halves[:, 1], halves[:, 0])
        held = keep + swap_bit(send, size, bit).astype(F32)
    return held[0]


def sinusoid(steps_given, width):
    half = width // 2
    freqs = jnp.exp(-math.log(10000.0) * jnp.arange(half, dtype=F32) / half)
    angles = steps_given.astype(F32)[..., None] * freqs
    return jnp.concatenate([jnp.sin(angles), jnp.cos(angles)], axis=-1)


def norm_parts(values):
    center = values - jnp.mean(values, axis=-1, keepdims=True)
    rate = lax.rsqrt(jnp.mean(center * center, axis=-1, keepdims=True) + epsilon)
    return center * rate, rate


def norm_pull(grad, xhat, rate, gain):
    c = grad * gain
    return rate * (
        c - jnp.mean(c, axis=-1, keepdims=True) - xhat * jnp.mean(c * xhat, axis=-1, keepdims=True)
    )


def gelu_both(values):
    cdf = 0.5 * (1.0 + lax.erf(values * math.sqrt(0.5)))
    slope = cdf + values * (jnp.exp(-0.5 * values * values) * (1.0 / math.sqrt(2.0 * math.pi)))
    return (values * cdf).astype(LOW), slope.astype(LOW)


def rows_dot(left, right):
    return dot32(left, right, (((0,), (0,)), ((), ())))


def column_sums(values):
    return rows_dot(jnp.ones((values.shape[0], 8), LOW), values)[0]


def take_half(values, which, axis):
    size = values.shape[axis] // 2
    return lax.dynamic_slice_in_dim(values, which * size, size, axis)


def per_device(
    tokens, timesteps, lengths, time_weight, attn_gain, attn_shift, qkv_weight, out_weight,
    out_bias, mlp_gain, mlp_shift, up_weight, up_bias, down_weight, down_bias, cotangent, *, size
):
    local = tokens.shape[1]
    width = tokens.shape[2]
    half = width // 2
    wide = up_weight.shape[1]
    shard = time_weight.shape[0]
    deep = down_weight.shape[0]
    spot = lax.axis_index("seq")
    row = lax.axis_index("dp")
    chip = spot // 2
    core = spot % 2
    on_one = core == 1

    def natural(own, other, axis):
        return jnp.where(
            on_one,
            jnp.concatenate([other, own], axis=axis),
            jnp.concatenate([own, other], axis=axis),
        )

    up_pairs = up_weight.astype(LOW).reshape(shard, size, 2, deep // 2)
    up_shard = lax.dynamic_index_in_dim(up_pairs, core, 2, False).reshape(shard, wide // 2)
    down_shard = take_half(down_weight.astype(LOW), core, 0)
    out_shard = take_half(out_weight.astype(LOW), core, 1)
    packed = jnp.concatenate(
        [
            up_shard[:, :width],
            up_shard[:, width:],
            down_shard,
            jnp.concatenate([out_shard[: shard // 2], out_shard[shard // 2 :]], axis=1),
        ],
        axis=0,
    )
    pack_rows = packed.shape[0]
    own_pack = lax.all_gather(packed, "dp", axis=0, tiled=False)
    other_pack = swap_core(own_pack)

    def unpack(pack):
        a = pack[:, :shard].reshape(width, width)
        b = pack[:, shard : 2 * shard].reshape(width, width)
        up = jnp.concatenate([a, b], axis=1)
        down = pack[:, 2 * shard : 2 * shard + deep // 2].reshape(wide // 2, width)
        last = pack[:, 2 * shard + deep // 2 :]
        out = jnp.concatenate([last[:, :, :half], last[:, :, half:]], axis=1).reshape(width, half)
        return up, down, out

    mine = lax.dynamic_index_in_dim(tokens, chip, 0, False)
    source = jnp.concatenate(
        [mine, swap_chip(lax.dynamic_index_in_dim(tokens, 1 - chip, 0, False))], axis=0
    )
    vectors = jnp.concatenate(
        [attn_gain, attn_shift, out_bias, mlp_gain, mlp_shift, down_bias, up_bias]
    ).astype(LOW).astype(F32)
    small = gather_dp(jnp.concatenate([timesteps.astype(F32), vectors])[None], size)[:, 0]
    steps = small[:, :2]
    gain_a, shift_a, bias_out, gain_m, shift_m, bias_down = [
        small[:, 2 + k * shard : 2 + (k + 1) * shard].reshape(width) for k in range(6)
    ]
    bias_up = small[:, 2 + 6 * shard :].reshape(size, 2, deep // 2)
    qkv_shard = lax.dynamic_index_in_dim(
        qkv_weight.astype(LOW).reshape(shard, 3, 2, half), core, 2, False
    ).reshape(shard, 3 * half)
    qkv_own = gather_dp(qkv_shard, size).reshape(width, 3 * half)

    embedded = sinusoid(steps, width).astype(LOW)
    embedded = jnp.where(chip == 1, embedded[:, ::-1], embedded)
    own_rows = lax.dynamic_slice_in_dim(embedded, row * shard, shard, 2)
    time_parts = jnp.dot(own_rows[:, 0], time_weight.astype(LOW), preferred_element_type=F32)
    time_shift = scatter_dp(time_parts[:, None], size, F32)

    length = lax.dynamic_index_in_dim(lengths, chip, 0, False)
    places = jnp.arange(local, dtype=jnp.int32)

    def positions(which):
        return jnp.concatenate(
            [(2 * chip + which) * local + places, (2 * (1 - chip) + which) * local + places]
        )

    own_places = positions(core)
    valid = (own_places < length)[:, None]
    bias = jnp.where(
        jnp.concatenate([own_places, positions(1 - core)]) < length, 0.0, -1e30
    ).astype(F32)[:, None]

    hidden = source + time_shift
    xhat_a, rate_a = norm_parts(hidden)
    normed_own = (xhat_a * gain_a + shift_a).astype(LOW)
    normed_all = jnp.concatenate([normed_own, swap_core(normed_own)], axis=0)
    projected = jnp.dot(normed_all, qkv_own, preferred_element_type=F32).astype(LOW)
    mixed, logs = attention_forward(projected, bias)
    count = hidden.shape[0]
    attended = natural(mixed[:count], swap_core(mixed[count:]), 1)

    cot_mine = lax.dynamic_index_in_dim(cotangent, chip, 0, False)
    cot = jnp.concatenate(
        [cot_mine, swap_chip(lax.dynamic_index_in_dim(cotangent, 1 - chip, 0, False))], axis=0
    )
    up_a, down_a, out_a = unpack(own_pack)
    up_b, down_b, out_b = unpack(other_pack)
    bias_up_a = lax.dynamic_index_in_dim(bias_up, core, 1, False).reshape(wide // 2)
    bias_up_b = lax.dynamic_index_in_dim(bias_up, 1 - core, 1, False).reshape(wide // 2)
    out_full = natural(out_a, out_b, 1)

    middle = hidden + jnp.dot(attended, out_full, preferred_element_type=F32) + bias_out
    xhat_m, rate_m = norm_parts(middle)
    normed_two = (xhat_m * gain_m + shift_m).astype(LOW)
    act_a, slope_a = gelu_both(jnp.dot(normed_two, up_a, preferred_element_type=F32) + bias_up_a)
    act_b, slope_b = gelu_both(jnp.dot(normed_two, up_b, preferred_element_type=F32) + bias_up_b)
    branch = (
        jnp.dot(act_a, down_a, preferred_element_type=F32)
        + jnp.dot(act_b, down_b, preferred_element_type=F32)
        + bias_down
    )
    result = jnp.where(valid, middle + branch, 0.0)

    grad_out = jnp.where(valid, cot, 0.0)
    grad_low = grad_out.astype(LOW)
    pre_a = (dot32(grad_low, down_a, NT) * slope_a.astype(F32)).astype(LOW)
    pre_b = (dot32(grad_low, down_b, NT) * slope_b.astype(F32)).astype(LOW)
    pre_a, pre_b = lax.optimization_barrier((pre_a, pre_b))
    grad_normed_two = dot32(pre_a, up_a, NT) + dot32(pre_b, up_b, NT)
    grad_middle = grad_out + norm_pull(grad_normed_two, xhat_m, rate_m, gain_m)
    grad_branch = grad_middle.astype(LOW)
    grad_attended = dot32(grad_branch, out_full, NT).astype(LOW)
    low_half, high_half = grad_attended[:, :half], grad_attended[:, half:]
    heads_own = jnp.where(on_one, high_half, low_half)
    heads_other = swap_core(jnp.where(on_one, low_half, high_half))
    grad_heads = jnp.concatenate([heads_own, heads_other], axis=0)

    def pack_grads(up, down, out):
        parts = [
            up[:, :width].reshape(size, shard, width),
            up[:, width:].reshape(size, shard, width),
            down.reshape(size, deep // 2, width),
        ]
        last = out.reshape(size, shard, half)
        parts.append(jnp.concatenate([last[:, : shard // 2], last[:, shard // 2 :]], axis=2))
        return jnp.concatenate([part.astype(LOW) for part in parts], axis=1)

    out_grad = rows_dot(attended, grad_branch)
    out_low, out_high = out_grad[:, :half], out_grad[:, half:]
    grads_a = pack_grads(
        rows_dot(normed_two, pre_a), rows_dot(act_a, grad_low), jnp.where(on_one, out_high, out_low)
    )
    grads_b = pack_grads(
        rows_dot(normed_two, pre_b), rows_dot(act_b, grad_low), jnp.where(on_one, out_low, out_high)
    )
    summed = (grads_a.astype(F32) + swap_core(grads_b).astype(F32)).astype(LOW)
    shards = lax.psum_scatter(summed, "dp", scatter_dimension=0, tiled=False)

    dq, dk, dv = attention_backward(projected, mixed, grad_heads, logs, bias)
    grad_projected = jnp.concatenate([dq, dk, dv], axis=1)
    part = dot32(grad_projected, qkv_own, NT)
    grad_normed_one = part[:count] + swap_core(part[count:].astype(LOW)).astype(F32)
    tokens_grad = grad_middle + norm_pull(grad_normed_one, xhat_a, rate_a, gain_a)

    qkv_grad = rows_dot(normed_all, grad_projected).reshape(size, shard, 3 * half)
    qkv_mine = scatter_dp(qkv_grad, size, LOW)
    qkv_mine = qkv_mine + swap_chip(qkv_mine.astype(LOW)).astype(F32)
    qkv_other = swap_core(qkv_mine.astype(LOW)).astype(F32)
    qkv_out = natural(
        qkv_mine.reshape(shard, 3, 1, half), qkv_other.reshape(shard, 3, 1, half), 2
    ).reshape(shard, 6 * half)

    sum_bias_up = natural(
        column_sums(pre_a).reshape(size, 1, deep // 2),
        column_sums(pre_b).reshape(size, 1, deep // 2),
        1,
    ).reshape(size, deep)
    vector_sums = jnp.concatenate(
        [
            jnp.sum(grad_normed_one * xhat_a, axis=0).reshape(size, shard),
            jnp.sum(grad_normed_one, axis=0).reshape(size, shard),
            column_sums(grad_branch).reshape(size, shard),
            jnp.sum(grad_normed_two * xhat_m, axis=0).reshape(size, shard),
            jnp.sum(grad_normed_two, axis=0).reshape(size, shard),
            column_sums(grad_low).reshape(size, shard),
            sum_bias_up,
        ],
        axis=1,
    )
    vector_mine = scatter_dp(vector_sums[:, None], size, F32)
    vector_mine = vector_mine + swap_core(vector_mine)
    vector_mine = (vector_mine + swap_chip(vector_mine))[0]
    vector_out = [vector_mine[k * shard : (k + 1) * shard] for k in range(6)]

    token_sum = jnp.sum(tokens_grad, axis=0, keepdims=True)
    token_sum = token_sum + swap_core(token_sum)
    sums_own = gather_dp(token_sum, size)[:, 0]
    sums_other = swap_chip(sums_own)
    exact = dict(precision=lax.Precision.HIGHEST, preferred_element_type=F32)
    contract = (((0,), (0,)), ((), ()))
    time_grad = lax.dot_general(
        own_rows[:, 0].astype(F32), sums_own, contract, **exact
    ) + lax.dot_general(own_rows[:, 1].astype(F32), sums_other, contract, **exact)

    shards = shards.astype(F32)
    shards = shards + swap_chip(shards.astype(LOW)).astype(F32)
    shards_other = swap_core(shards.astype(LOW)).astype(F32)

    def unpack_grads(pack):
        up = jnp.concatenate([pack[:shard], pack[shard : 2 * shard]], axis=1)
        down = pack[2 * shard : 2 * shard + deep // 2]
        last = pack[2 * shard + deep // 2 :]
        return up, down, jnp.concatenate([last[:, :half], last[:, half:]], axis=0)

    up_ga, down_ga, out_ga = unpack_grads(shards)
    up_gb, down_gb, out_gb = unpack_grads(shards_other)
    up_out = natural(
        up_ga.reshape(shard, size, 1, deep // 2), up_gb.reshape(shard, size, 1, deep // 2), 2
    ).reshape(shard, wide)

    def hand_back(values):
        kept = values[:local]
        got = swap_chip(values[local:])
        return jnp.where(chip == 1, jnp.stack([got, kept]), jnp.stack([kept, got]))

    return (
        hand_back(result),
        hand_back(tokens_grad),
        time_grad,
        vector_out[0],
        vector_out[1],
        qkv_out,
        natural(out_ga, out_gb, 1),
        vector_out[2],
        vector_out[3],
        vector_out[4],
        up_out,
        vector_mine[6 * shard :],
        natural(down_ga, down_gb, 0),
        vector_out[5],
    )


def solution(mesh):
    batch = P("dp", "seq", None)
    flat = P("dp")
    grid = P("dp", None)
    in_specs = (
        batch, flat, flat, grid, flat, flat, grid, grid, flat, flat, flat, grid, flat, grid, flat,
        batch,
    )
    out_specs = (
        batch, batch, grid, flat, flat, grid, grid, flat, flat, flat, grid, flat, grid, flat,
    )
    body = functools.partial(per_device, size=mesh.shape["dp"])
    return jax.shard_map(
        body, mesh=mesh, in_specs=in_specs, out_specs=out_specs, check_vma=False
    )
```

```python
import functools, math
import jax, jax.numpy as jnp
from jax import lax
from jax.experimental import pallas as pl
from jax.experimental.pallas import tpu as pltpu
from jax.sharding import PartitionSpec as P


HEAD = 64
PAIR = 2 * HEAD
NT = (((1,), (1,)), ((), ()))
NN = (((1,), (0,)), ((), ()))
SCALE = 1.0 / math.sqrt(HEAD)


def dot32(left, right, dims):
    return lax.dot_general(left, right, dims, preferred_element_type=jnp.float32)


def one_head(block, which):
    lane = lax.broadcasted_iota(jnp.int32, block.shape, 1)
    return jnp.where(lane // HEAD == which, block.astype(jnp.float32), 0.0)


def attention_forward_kernel(bias_ref, q_ref, k_ref, v_ref, out_ref, wide_ref, log_ref, vt_ref, *, chunk):
    @pl.when(pl.program_id(1) == 0)
    def _():
        vt_ref[...] = v_ref[...].T

    total = k_ref.shape[0]
    mixed = []
    for which in range(2):
        query = (one_head(q_ref[...], which) * SCALE).astype(jnp.bfloat16)
        scores = []
        for start in range(0, total, chunk):
            rows = pl.ds(start, chunk)
            part = dot32(k_ref[rows, :], query, NT) + bias_ref[rows, :]
            scores.append(part)
        top = jnp.max(scores[0], axis=0, keepdims=True)
        for part in scores[1:]:
            top = jnp.maximum(top, jnp.max(part, axis=0, keepdims=True))
        totals = 0.0
        acc = 0.0
        for index, part in enumerate(scores):
            weights = jnp.exp(part - top)
            totals = totals + jnp.sum(weights, axis=0, keepdims=True)
            values = vt_ref[which * HEAD : (which + 1) * HEAD, index * chunk : (index + 1) * chunk]
            acc = acc + dot32(values, weights.astype(jnp.bfloat16), NN)
        mixed.append(acc / totals)
        log_ref[0, which : which + 1, :] = top + jnp.log(totals)
    joined = jnp.concatenate(mixed, axis=0)
    wide_ref[0] = joined
    out_ref[...] = joined.T.astype(jnp.bfloat16)


def attention_backward_kernel(
    bias_ref, q_ref, k_ref, v_ref, mixed_ref, grad_ref, log_ref,
    dq_ref, dk_ref, dv_ref, kt_ref, dk_acc, dv_acc, *, chunk
):
    step = pl.program_id(1)

    @pl.when(step == 0)
    def _():
        kt_ref[...] = k_ref[...].T
        dk_acc[...] = jnp.zeros_like(dk_acc)
        dv_acc[...] = jnp.zeros_like(dv_acc)

    total = k_ref.shape[0]
    centre_t = grad_ref[...].astype(jnp.float32).T * mixed_ref[0]
    queries = []
    grads = []
    for which in range(2):
        queries.append((one_head(q_ref[...], which) * SCALE).astype(jnp.bfloat16))
        grads.append(one_head(grad_ref[...], which).astype(jnp.bfloat16))
    dq_parts = [0.0, 0.0]
    for start in range(0, total, chunk):
        rows = pl.ds(start, chunk)
        dk_part = dk_acc[rows, :]
        dv_part = dv_acc[rows, :]
        for which in range(2):
            head = slice(which * HEAD, (which + 1) * HEAD)
            centre = jnp.sum(centre_t[head, :], axis=0, keepdims=True)
            scores = dot32(k_ref[rows, :], queries[which], NT) + bias_ref[rows, :]
            probs = jnp.exp(scores - log_ref[0, which : which + 1, :])
            grad_probs = dot32(v_ref[rows, :], grads[which], NT)
            grad_scores = (probs * (grad_probs - centre)).astype(jnp.bfloat16)
            dv_part = dv_part + dot32(probs.astype(jnp.bfloat16), grads[which], NN)
            dk_part = dk_part + dot32(grad_scores, queries[which], NN)
            dq_parts[which] = dq_parts[which] + dot32(
                kt_ref[head, start : start + chunk], grad_scores, NN
            )
        dk_acc[rows, :] = dk_part
        dv_acc[rows, :] = dv_part
    dq_ref[...] = (jnp.concatenate(dq_parts, axis=0).T * SCALE).astype(jnp.bfloat16)

    @pl.when(step == pl.num_programs(1) - 1)
    def _():
        dk_ref[...] = dk_acc[...].astype(jnp.bfloat16)
        dv_ref[...] = dv_acc[...].astype(jnp.bfloat16)


def cost_of(total, pairs, products):
    return pl.CostEstimate(
        flops=pairs * 2 * products * 2 * total * total * 4 * HEAD,
        transcendentals=pairs * 2 * total * total,
        bytes_accessed=pairs * total * PAIR * 16,
    )


def attention_forward(projected, bias, first, pairs, block=512, chunk=512):
    total = projected.shape[0]
    every = projected.shape[1] // (3 * PAIR)
    block = min(block, total)
    return pl.pallas_call(
        functools.partial(attention_forward_kernel, chunk=min(chunk, total)),
        name="attention_forward",
        cost_estimate=cost_of(total, pairs, 2),
        grid=(pairs, total // block),
        in_specs=[
            pl.BlockSpec((total, 1), lambda p, i: (0, 0)),
            pl.BlockSpec((block, PAIR), lambda p, i: (i, first + p)),
            pl.BlockSpec((total, PAIR), lambda p, i: (0, every + first + p)),
            pl.BlockSpec((total, PAIR), lambda p, i: (0, 2 * every + first + p)),
        ],
        out_specs=[
            pl.BlockSpec((block, PAIR), lambda p, i: (i, p)),
            pl.BlockSpec((1, PAIR, block), lambda p, i: (p, 0, i)),
            pl.BlockSpec((1, 2, block), lambda p, i: (p, 0, i)),
        ],
        out_shape=[
            jax.ShapeDtypeStruct((total, pairs * PAIR), jnp.bfloat16),
            jax.ShapeDtypeStruct((pairs, PAIR, total), jnp.float32),
            jax.ShapeDtypeStruct((pairs, 2, total), jnp.float32),
        ],
        scratch_shapes=[pltpu.VMEM((PAIR, total), jnp.bfloat16)],
    )(bias, projected, projected, projected)


def attention_backward(projected, mixed, grad_mixed, logs, bias, first, block=512, chunk=256):
    total = projected.shape[0]
    every = projected.shape[1] // (3 * PAIR)
    pairs = mixed.shape[0]
    block = min(block, total)
    out = jax.ShapeDtypeStruct((total, pairs * PAIR), jnp.bfloat16)
    return pl.pallas_call(
        functools.partial(attention_backward_kernel, chunk=min(chunk, total)),
        name="attention_backward",
        cost_estimate=cost_of(total, pairs, 5),
        grid=(pairs, total // block),
        in_specs=[
            pl.BlockSpec((total, 1), lambda p, i: (0, 0)),
            pl.BlockSpec((block, PAIR), lambda p, i: (i, first + p)),
            pl.BlockSpec((total, PAIR), lambda p, i: (0, every + first + p)),
            pl.BlockSpec((total, PAIR), lambda p, i: (0, 2 * every + first + p)),
            pl.BlockSpec((1, PAIR, block), lambda p, i: (p, 0, i)),
            pl.BlockSpec((block, PAIR), lambda p, i: (i, first + p)),
            pl.BlockSpec((1, 2, block), lambda p, i: (p, 0, i)),
        ],
        out_specs=[
            pl.BlockSpec((block, PAIR), lambda p, i: (i, p)),
            pl.BlockSpec((total, PAIR), lambda p, i: (0, p)),
            pl.BlockSpec((total, PAIR), lambda p, i: (0, p)),
        ],
        out_shape=[out, out, out],
        scratch_shapes=[
            pltpu.VMEM((PAIR, total), jnp.bfloat16),
            pltpu.VMEM((total, PAIR), jnp.float32),
            pltpu.VMEM((total, PAIR), jnp.float32),
        ],
    )(bias, projected, projected, projected, mixed, grad_mixed, logs)


epsilon = 1e-05

CORE_SWAP = ((0, 1), (1, 0), (2, 3), (3, 2))
CHIP_SWAP = ((0, 2), (2, 0), (1, 3), (3, 1))
LOW = jnp.bfloat16
F32 = jnp.float32


def swap_core(values):
    return lax.ppermute(values, "seq", CORE_SWAP)


def swap_chip(values):
    return lax.ppermute(values, "seq", CHIP_SWAP)


def swap_bit(values, size, bit):
    return lax.ppermute(values, "dp", [(i, i ^ bit) for i in range(size)])


def bits_of(size):
    return [1 << b for b in range(size.bit_length() - 1)]


def gather_dp(values, size):
    me = lax.axis_index("dp")
    held = values[None]
    for bit in reversed(bits_of(size)):
        got = swap_bit(held, size, bit)
        upper = (me & bit) != 0
        first = jnp.where(upper, got, held)
        second = jnp.where(upper, held, got)
        held = jnp.stack([first, second], axis=1).reshape((-1,) + values.shape)
    return held


def scatter_dp(values, size, wire):
    me = lax.axis_index("dp")
    held = values
    for bit in bits_of(size):
        upper = (me & bit) != 0
        halves = held.reshape((held.shape[0] // 2, 2) + held.shape[1:])
        send = jnp.where(upper, halves[:, 0], halves[:, 1]).astype(wire)
        keep = jnp.where(upper, halves[:, 1], halves[:, 0])
        held = keep + swap_bit(send, size, bit).astype(F32)
    return held[0]


def sinusoid(steps_given, width):
    half = width // 2
    freqs = jnp.exp(-math.log(10000.0) * jnp.arange(half, dtype=F32) / half)
    angles = steps_given.astype(F32)[..., None] * freqs
    return jnp.concatenate([jnp.sin(angles), jnp.cos(angles)], axis=-1)


def norm_parts(values):
    center = values - jnp.mean(values, axis=-1, keepdims=True)
    rate = lax.rsqrt(jnp.mean(center * center, axis=-1, keepdims=True) + epsilon)
    return center * rate, rate


def norm_pull(grad, xhat, rate, gain):
    c = grad * gain
    return rate * (
        c - jnp.mean(c, axis=-1, keepdims=True) - xhat * jnp.mean(c * xhat, axis=-1, keepdims=True)
    )


def gelu_both(values):
    cdf = 0.5 * (1.0 + lax.erf(values * math.sqrt(0.5)))
    slope = cdf + values * (jnp.exp(-0.5 * values * values) * (1.0 / math.sqrt(2.0 * math.pi)))
    return (values * cdf).astype(LOW), slope.astype(LOW)


def rows_dot(left, right):
    return dot32(left, right, (((0,), (0,)), ((), ())))


def column_sums(values):
    return rows_dot(jnp.ones((values.shape[0], 8), LOW), values)[0]


def take_half(values, which, axis):
    size = values.shape[axis] // 2
    return lax.dynamic_slice_in_dim(values, which * size, size, axis)


def layer(
    tokens, timesteps, lengths, time_weight, attn_gain, attn_shift, qkv_weight, out_weight,
    out_bias, mlp_gain, mlp_shift, up_weight, up_bias, down_weight, down_bias, cotangent, *, size
):
    local = tokens.shape[1]
    width = tokens.shape[2]
    half = width // 2
    wide = up_weight.shape[1]
    shard = time_weight.shape[0]
    deep = down_weight.shape[0]
    spot = lax.axis_index("seq")
    row = lax.axis_index("dp")
    chip = spot // 2
    core = spot % 2
    on_one = core == 1

    def natural(own, other, axis):
        return jnp.where(
            on_one,
            jnp.concatenate([other, own], axis=axis),
            jnp.concatenate([own, other], axis=axis),
        )

    pieces = [qkv_weight[:, k * half : (k + 1) * half] for k in range(6)]
    qkv_shard = jnp.where(
        on_one, jnp.concatenate(pieces[1::2], axis=1), jnp.concatenate(pieces[0::2], axis=1)
    ).astype(LOW)
    vectors = jnp.concatenate(
        [attn_gain, attn_shift, out_bias, mlp_gain, mlp_shift, down_bias, up_bias]
    ).astype(LOW).astype(F32)
    vectors = jnp.concatenate([timesteps.astype(F32), vectors])[None]
    qkv_shard, vectors, tokens, time_weight, up_weight, down_weight, out_weight = (
        lax.optimization_barrier(
            (qkv_shard, vectors, tokens, time_weight, up_weight, down_weight, out_weight)
        )
    )
    qkv_own = gather_dp(qkv_shard, size).reshape(width, 3 * half)

    up_pairs = up_weight.astype(LOW).reshape(shard, size, 2, deep // 2)
    up_shard = lax.dynamic_index_in_dim(up_pairs, core, 2, False).reshape(shard, wide // 2)
    down_shard = take_half(down_weight.astype(LOW), core, 0)
    out_shard = take_half(out_weight.astype(LOW), core, 1)
    packed = jnp.concatenate(
        [
            up_shard[:, :width],
            up_shard[:, width:],
            down_shard,
            jnp.concatenate([out_shard[: shard // 2], out_shard[shard // 2 :]], axis=1),
        ],
        axis=0,
    )
    own_pack = lax.all_gather(packed, "dp", axis=0, tiled=False)

    def unpack(pack):
        a = pack[:, :shard].reshape(width, width)
        b = pack[:, shard : 2 * shard].reshape(width, width)
        up = jnp.concatenate([a, b], axis=1)
        down = pack[:, 2 * shard : 2 * shard + deep // 2].reshape(wide // 2, width)
        last = pack[:, 2 * shard + deep // 2 :]
        out = jnp.concatenate([last[:, :, :half], last[:, :, half:]], axis=1).reshape(width, half)
        return up, down, out

    mine = lax.dynamic_index_in_dim(tokens, chip, 0, False)
    source = jnp.concatenate(
        [mine, swap_chip(lax.dynamic_index_in_dim(tokens, 1 - chip, 0, False))], axis=0
    )
    small = gather_dp(vectors, size)[:, 0]
    steps = small[:, :2]
    gain_a, shift_a, bias_out, gain_m, shift_m, bias_down = [
        small[:, 2 + k * shard : 2 + (k + 1) * shard].reshape(width) for k in range(6)
    ]
    bias_up = small[:, 2 + 6 * shard :].reshape(size, 2, deep // 2)
    embedded = sinusoid(steps, width).astype(LOW)
    embedded = jnp.where(chip == 1, embedded[:, ::-1], embedded)
    own_rows = lax.dynamic_slice_in_dim(embedded, row * shard, shard, 2)
    time_parts = jnp.dot(own_rows[:, 0], time_weight.astype(LOW), preferred_element_type=F32)
    time_shift = scatter_dp(time_parts[:, None], size, F32)

    length = lax.dynamic_index_in_dim(lengths, chip, 0, False)
    places = jnp.arange(local, dtype=jnp.int32)

    def positions(which):
        return jnp.concatenate(
            [(2 * chip + which) * local + places, (2 * (1 - chip) + which) * local + places]
        )

    own_places = positions(core)
    valid = (own_places < length)[:, None]
    bias = jnp.where(
        jnp.concatenate([own_places, positions(1 - core)]) < length, 0.0, -1e30
    ).astype(F32)[:, None]

    hidden = source + time_shift
    xhat_a, rate_a = norm_parts(hidden)
    normed_own = (xhat_a * gain_a + shift_a).astype(LOW)
    normed_all = jnp.concatenate([normed_own, swap_core(normed_own)], axis=0)
    projected = jnp.dot(normed_all, qkv_own, preferred_element_type=F32).astype(LOW)
    projected, cotangent = lax.optimization_barrier((projected, cotangent))
    count = hidden.shape[0]
    lead = half // PAIR - 1
    mixed_one, wide_one, logs_one = attention_forward(projected, bias, 0, lead)
    mixed_one, own_pack, projected_late = lax.optimization_barrier((mixed_one, own_pack, projected))
    other_pack = swap_core(own_pack)
    sent_one = swap_core(mixed_one[count:])
    mixed_two, wide_two, logs_two = attention_forward(projected_late, bias, lead, 1)
    attended = natural(
        jnp.concatenate([mixed_one[:count], mixed_two[:count]], axis=1),
        jnp.concatenate([sent_one, swap_core(mixed_two[count:])], axis=1),
        1,
    )
    wide_mixed = jnp.concatenate([wide_one, wide_two], axis=0)
    logs = jnp.concatenate([logs_one, logs_two], axis=0)

    cot_mine = lax.dynamic_index_in_dim(cotangent, chip, 0, False)
    cot_send = lax.dynamic_index_in_dim(cotangent, 1 - chip, 0, False)
    cot = jnp.concatenate([cot_mine, swap_chip(cot_send)], axis=0)
    up_a, down_a, out_a = unpack(own_pack)
    up_b, down_b, out_b = unpack(other_pack)
    bias_up_a = lax.dynamic_index_in_dim(bias_up, core, 1, False).reshape(wide // 2)
    bias_up_b = lax.dynamic_index_in_dim(bias_up, 1 - core, 1, False).reshape(wide // 2)
    out_full = natural(out_a, out_b, 1)

    middle = hidden + jnp.dot(attended, out_full, preferred_element_type=F32) + bias_out
    xhat_m, rate_m = norm_parts(middle)
    normed_two = (xhat_m * gain_m + shift_m).astype(LOW)
    act_a, slope_a = gelu_both(jnp.dot(normed_two, up_a, preferred_element_type=F32) + bias_up_a)
    act_b, slope_b = gelu_both(jnp.dot(normed_two, up_b, preferred_element_type=F32) + bias_up_b)
    branch = (
        jnp.dot(act_a, down_a, preferred_element_type=F32)
        + jnp.dot(act_b, down_b, preferred_element_type=F32)
        + bias_down
    )
    result = jnp.where(valid, middle + branch, 0.0)

    grad_out = jnp.where(valid, cot, 0.0)
    grad_low = grad_out.astype(LOW)
    pre_a = (dot32(grad_low, down_a, NT) * slope_a.astype(F32)).astype(LOW)
    pre_b = (dot32(grad_low, down_b, NT) * slope_b.astype(F32)).astype(LOW)
    pre_a, pre_b = lax.optimization_barrier((pre_a, pre_b))
    grad_normed_two = dot32(pre_a, up_a, NT) + dot32(pre_b, up_b, NT)
    grad_middle = grad_out + norm_pull(grad_normed_two, xhat_m, rate_m, gain_m)
    grad_branch = grad_middle.astype(LOW)
    grad_attended = dot32(grad_branch, out_full, NT).astype(LOW)
    low_half, high_half = grad_attended[:, :half], grad_attended[:, half:]
    heads_own = jnp.where(on_one, high_half, low_half)
    heads_other = swap_core(jnp.where(on_one, low_half, high_half))
    grad_heads = jnp.concatenate([heads_own, heads_other], axis=0)

    def pack_grads(up, down, out):
        parts = [
            up[:, :width].reshape(size, shard, width),
            up[:, width:].reshape(size, shard, width),
            down.reshape(size, deep // 2, width),
        ]
        last = out.reshape(size, shard, half)
        parts.append(jnp.concatenate([last[:, : shard // 2], last[:, shard // 2 :]], axis=2))
        return jnp.concatenate([part.astype(LOW) for part in parts], axis=1)

    out_grad = rows_dot(attended, grad_branch)
    out_low, out_high = out_grad[:, :half], out_grad[:, half:]
    grads_a = pack_grads(
        rows_dot(normed_two, pre_a), rows_dot(act_a, grad_low), jnp.where(on_one, out_high, out_low)
    )
    grads_b = pack_grads(
        rows_dot(normed_two, pre_b), rows_dot(act_b, grad_low), jnp.where(on_one, out_low, out_high)
    )
    summed = (grads_a.astype(F32) + swap_core(grads_b).astype(F32)).astype(LOW)
    grad_heads, summed = lax.optimization_barrier((grad_heads, summed))
    shards = lax.psum_scatter(summed, "dp", scatter_dimension=0, tiled=False)
    dq, dk, dv = attention_backward(projected, wide_mixed, grad_heads, logs, bias, 0)
    grad_projected = jnp.concatenate([dq, dk, dv], axis=1)
    part_other = swap_core(dot32(grad_projected[count:], qkv_own, NT).astype(LOW))
    grad_projected, part_other = lax.optimization_barrier((grad_projected, part_other))
    qkv_grad = rows_dot(normed_all, grad_projected).reshape(size, 2, shard // 2, 3 * half)
    on_chip_one = chip == 1
    qkv_keep = jnp.where(on_chip_one, qkv_grad[:, 1], qkv_grad[:, 0])
    qkv_send = jnp.where(on_chip_one, qkv_grad[:, 0], qkv_grad[:, 1]).astype(LOW)
    qkv_mine = scatter_dp(qkv_keep + swap_chip(qkv_send).astype(F32), size, LOW)
    qkv_more = swap_chip(qkv_mine)
    qkv_mine = jnp.where(
        on_chip_one,
        jnp.concatenate([qkv_more, qkv_mine], axis=0),
        jnp.concatenate([qkv_mine, qkv_more], axis=0),
    )
    qkv_other = swap_core(qkv_mine)
    qkv_out = jnp.concatenate(
        [
            natural(
                qkv_mine[:, k * half : (k + 1) * half], qkv_other[:, k * half : (k + 1) * half], 1
            )
            for k in range(3)
        ],
        axis=1,
    )

    part_own = dot32(grad_projected[:count], qkv_own, NT)
    grad_normed_one = part_own + part_other.astype(F32)
    tokens_grad = grad_middle + norm_pull(grad_normed_one, xhat_a, rate_a, gain_a)

    sum_bias_up = natural(
        column_sums(pre_a).reshape(size, 1, deep // 2),
        column_sums(pre_b).reshape(size, 1, deep // 2),
        1,
    ).reshape(size, deep)
    vector_sums = jnp.concatenate(
        [
            jnp.sum(grad_normed_one * xhat_a, axis=0).reshape(size, shard),
            jnp.sum(grad_normed_one, axis=0).reshape(size, shard),
            column_sums(grad_branch).reshape(size, shard),
            jnp.sum(grad_normed_two * xhat_m, axis=0).reshape(size, shard),
            jnp.sum(grad_normed_two, axis=0).reshape(size, shard),
            column_sums(grad_low).reshape(size, shard),
            sum_bias_up,
        ],
        axis=1,
    )
    token_sum = jnp.sum(tokens_grad, axis=0, keepdims=True)
    sums = jnp.concatenate([vector_sums.reshape(1, -1), token_sum], axis=1)
    sums = sums + swap_core(sums)
    sums_there = swap_chip(sums)
    tokens_grad, sums_there = lax.optimization_barrier((tokens_grad, sums_there))
    vector_sums = (sums + sums_there)[:, : vector_sums.size].reshape(vector_sums.shape)
    vector_mine = scatter_dp(vector_sums[:, None], size, F32)[0]
    vector_out = [vector_mine[k * shard : (k + 1) * shard] for k in range(6)]
    both = jnp.concatenate([sums, sums_there], axis=0)[:, -width:]
    gathered = gather_dp(both, size)
    sums_own = gathered[:, 0]
    sums_other = gathered[:, 1]
    exact = dict(precision=lax.Precision.HIGHEST, preferred_element_type=F32)
    contract = (((0,), (0,)), ((), ()))
    time_grad = lax.dot_general(
        own_rows[:, 0].astype(F32), sums_own, contract, **exact
    ) + lax.dot_general(own_rows[:, 1].astype(F32), sums_other, contract, **exact)

    shards = shards.astype(F32)
    shards = shards + swap_chip(shards.astype(LOW)).astype(F32)
    shards_other = swap_core(shards.astype(LOW)).astype(F32)

    def unpack_grads(pack):
        up = jnp.concatenate([pack[:shard], pack[shard : 2 * shard]], axis=1)
        down = pack[2 * shard : 2 * shard + deep // 2]
        last = pack[2 * shard + deep // 2 :]
        return up, down, jnp.concatenate([last[:, :half], last[:, half:]], axis=0)

    up_ga, down_ga, out_ga = unpack_grads(shards)
    up_gb, down_gb, out_gb = unpack_grads(shards_other)
    up_out = natural(
        up_ga.reshape(shard, size, 1, deep // 2), up_gb.reshape(shard, size, 1, deep // 2), 2
    ).reshape(shard, wide)

    def hand_back(values, wire):
        kept = values[:local]
        got = swap_chip(values[local:].astype(wire)).astype(F32)
        return jnp.where(chip == 1, jnp.stack([got, kept]), jnp.stack([kept, got]))

    return (
        hand_back(result, F32),
        hand_back(tokens_grad, LOW),
        time_grad,
        vector_out[0],
        vector_out[1],
        qkv_out,
        natural(out_ga, out_gb, 1),
        vector_out[2],
        vector_out[3],
        vector_out[4],
        up_out,
        vector_mine[6 * shard :],
        natural(down_ga, down_gb, 0),
        vector_out[5],
    )


def solution(mesh):
    batch = P("dp", "seq", None)
    flat = P("dp")
    grid = P("dp", None)
    in_specs = (
        batch, flat, flat, grid, flat, flat, grid, grid, flat, flat, flat, grid, flat, grid, flat,
        batch,
    )
    out_specs = (
        batch, batch, grid, flat, flat, grid, grid, flat, flat, flat, grid, flat, grid, flat,
    )
    body = functools.partial(layer, size=mesh.shape["dp"])
    return jax.shard_map(
        body, mesh=mesh, in_specs=in_specs, out_specs=out_specs, check_vma=False
    )
```

```python
import functools, math
import jax, jax.numpy as jnp
from jax import lax
from jax.experimental import pallas as pl
from jax.experimental.layout import Layout, with_layout_constraint
from jax.experimental.pallas import tpu as pltpu
from jax.sharding import PartitionSpec as P


HEAD = 64
PAIR = 2 * HEAD
NT = (((1,), (1,)), ((), ()))
NN = (((1,), (0,)), ((), ()))
SCALE = 1.0 / math.sqrt(HEAD)


def dot32(left, right, dims):
    return lax.dot_general(left, right, dims, preferred_element_type=jnp.float32)


def one_head(block, which):
    lane = lax.broadcasted_iota(jnp.int32, block.shape, 1)
    return jnp.where(lane // HEAD == which, block.astype(jnp.float32), 0.0)


def attention_forward_kernel(bias_ref, q_ref, k_ref, v_ref, out_ref, wide_ref, log_ref, vt_ref, *, chunk):
    @pl.when(pl.program_id(1) == 0)
    def _():
        vt_ref[...] = v_ref[...].T

    total = k_ref.shape[0]
    mixed = []
    for which in range(2):
        query = (one_head(q_ref[...], which) * SCALE).astype(jnp.bfloat16)
        scores = []
        for start in range(0, total, chunk):
            rows = pl.ds(start, chunk)
            part = dot32(k_ref[rows, :], query, NT) + bias_ref[rows, :]
            scores.append(part)
        top = jnp.max(scores[0], axis=0, keepdims=True)
        for part in scores[1:]:
            top = jnp.maximum(top, jnp.max(part, axis=0, keepdims=True))
        totals = 0.0
        acc = 0.0
        for index, part in enumerate(scores):
            weights = jnp.exp(part - top)
            totals = totals + jnp.sum(weights, axis=0, keepdims=True)
            values = vt_ref[which * HEAD : (which + 1) * HEAD, index * chunk : (index + 1) * chunk]
            acc = acc + dot32(values, weights.astype(jnp.bfloat16), NN)
        mixed.append(acc / totals)
        log_ref[0, which : which + 1, :] = top + jnp.log(totals)
    joined = jnp.concatenate(mixed, axis=0)
    wide_ref[0] = joined
    out_ref[...] = joined.T.astype(jnp.bfloat16)


def attention_backward_kernel(
    bias_ref, q_ref, k_ref, v_ref, mixed_ref, grad_ref, log_ref,
    dq_ref, dk_ref, dv_ref, kt_ref, dk_acc, dv_acc, *, chunk
):
    step = pl.program_id(1)

    @pl.when(step == 0)
    def _():
        kt_ref[...] = k_ref[...].T
        dk_acc[...] = jnp.zeros_like(dk_acc)
        dv_acc[...] = jnp.zeros_like(dv_acc)

    total = k_ref.shape[0]
    centre_t = grad_ref[...].astype(jnp.float32).T * mixed_ref[0]
    queries = []
    grads = []
    for which in range(2):
        queries.append((one_head(q_ref[...], which) * SCALE).astype(jnp.bfloat16))
        grads.append(one_head(grad_ref[...], which).astype(jnp.bfloat16))
    dq_parts = [0.0, 0.0]
    for start in range(0, total, chunk):
        rows = pl.ds(start, chunk)
        dk_part = dk_acc[rows, :]
        dv_part = dv_acc[rows, :]
        for which in range(2):
            head = slice(which * HEAD, (which + 1) * HEAD)
            centre = jnp.sum(centre_t[head, :], axis=0, keepdims=True)
            scores = dot32(k_ref[rows, :], queries[which], NT) + bias_ref[rows, :]
            probs = jnp.exp(scores - log_ref[0, which : which + 1, :])
            grad_probs = dot32(v_ref[rows, :], grads[which], NT)
            grad_scores = (probs * (grad_probs - centre)).astype(jnp.bfloat16)
            dv_part = dv_part + dot32(probs.astype(jnp.bfloat16), grads[which], NN)
            dk_part = dk_part + dot32(grad_scores, queries[which], NN)
            dq_parts[which] = dq_parts[which] + dot32(
                kt_ref[head, start : start + chunk], grad_scores, NN
            )
        dk_acc[rows, :] = dk_part
        dv_acc[rows, :] = dv_part
    dq_ref[...] = (jnp.concatenate(dq_parts, axis=0).T * SCALE).astype(jnp.bfloat16)

    @pl.when(step == pl.num_programs(1) - 1)
    def _():
        dk_ref[...] = dk_acc[...].astype(jnp.bfloat16)
        dv_ref[...] = dv_acc[...].astype(jnp.bfloat16)


def cost_of(total, pairs, products):
    return pl.CostEstimate(
        flops=pairs * 2 * products * 2 * total * total * 4 * HEAD,
        transcendentals=pairs * 2 * total * total,
        bytes_accessed=pairs * total * PAIR * 16,
    )


def attention_forward(projected, bias, first, pairs, block=512, chunk=512):
    total = projected.shape[0]
    every = projected.shape[1] // (3 * PAIR)
    block = min(block, total)
    return pl.pallas_call(
        functools.partial(attention_forward_kernel, chunk=min(chunk, total)),
        name="attention_forward",
        cost_estimate=cost_of(total, pairs, 2),
        grid=(pairs, total // block),
        in_specs=[
            pl.BlockSpec((total, 1), lambda p, i: (0, 0)),
            pl.BlockSpec((block, PAIR), lambda p, i: (i, first + p)),
            pl.BlockSpec((total, PAIR), lambda p, i: (0, every + first + p)),
            pl.BlockSpec((total, PAIR), lambda p, i: (0, 2 * every + first + p)),
        ],
        out_specs=[
            pl.BlockSpec((block, PAIR), lambda p, i: (i, p)),
            pl.BlockSpec((1, PAIR, block), lambda p, i: (p, 0, i)),
            pl.BlockSpec((1, 2, block), lambda p, i: (p, 0, i)),
        ],
        out_shape=[
            jax.ShapeDtypeStruct((total, pairs * PAIR), jnp.bfloat16),
            jax.ShapeDtypeStruct((pairs, PAIR, total), jnp.float32),
            jax.ShapeDtypeStruct((pairs, 2, total), jnp.float32),
        ],
        scratch_shapes=[pltpu.VMEM((PAIR, total), jnp.bfloat16)],
    )(bias, projected, projected, projected)


def attention_backward(projected, mixed, grad_mixed, logs, bias, first, block=512, chunk=256):
    total = projected.shape[0]
    every = projected.shape[1] // (3 * PAIR)
    pairs = mixed.shape[0]
    block = min(block, total)
    out = jax.ShapeDtypeStruct((total, pairs * PAIR), jnp.bfloat16)
    return pl.pallas_call(
        functools.partial(attention_backward_kernel, chunk=min(chunk, total)),
        name="attention_backward",
        cost_estimate=cost_of(total, pairs, 5),
        grid=(pairs, total // block),
        in_specs=[
            pl.BlockSpec((total, 1), lambda p, i: (0, 0)),
            pl.BlockSpec((block, PAIR), lambda p, i: (i, first + p)),
            pl.BlockSpec((total, PAIR), lambda p, i: (0, every + first + p)),
            pl.BlockSpec((total, PAIR), lambda p, i: (0, 2 * every + first + p)),
            pl.BlockSpec((1, PAIR, block), lambda p, i: (p, 0, i)),
            pl.BlockSpec((block, PAIR), lambda p, i: (i, first + p)),
            pl.BlockSpec((1, 2, block), lambda p, i: (p, 0, i)),
        ],
        out_specs=[
            pl.BlockSpec((block, PAIR), lambda p, i: (i, p)),
            pl.BlockSpec((total, PAIR), lambda p, i: (0, p)),
            pl.BlockSpec((total, PAIR), lambda p, i: (0, p)),
        ],
        out_shape=[out, out, out],
        scratch_shapes=[
            pltpu.VMEM((PAIR, total), jnp.bfloat16),
            pltpu.VMEM((total, PAIR), jnp.float32),
            pltpu.VMEM((total, PAIR), jnp.float32),
        ],
    )(bias, projected, projected, projected, mixed, grad_mixed, logs)


epsilon = 1e-05

CORE_SWAP = ((0, 1), (1, 0), (2, 3), (3, 2))
CHIP_SWAP = ((0, 2), (2, 0), (1, 3), (3, 1))
LOW = jnp.bfloat16
F32 = jnp.float32


def swap_core(values):
    return lax.ppermute(values, "seq", CORE_SWAP)


def swap_chip(values):
    return lax.ppermute(values, "seq", CHIP_SWAP)


def swap_bit(values, size, bit):
    return lax.ppermute(values, "dp", [(i, i ^ bit) for i in range(size)])


def bits_of(size):
    return [1 << b for b in range(size.bit_length() - 1)]


def gather_step(held, size, bit):
    upper = (lax.axis_index("dp") & bit) != 0
    got = swap_bit(held, size, bit)
    first = jnp.where(upper, got, held)
    second = jnp.where(upper, held, got)
    return jnp.stack([first, second], axis=1).reshape((-1,) + held.shape[1:])


def gather_dp(values, size):
    held = values[None]
    for bit in reversed(bits_of(size)):
        held = gather_step(held, size, bit)
    return held


def scatter_dp(values, size, wire):
    me = lax.axis_index("dp")
    held = values
    for bit in bits_of(size):
        upper = (me & bit) != 0
        halves = held.reshape((held.shape[0] // 2, 2) + held.shape[1:])
        send = jnp.where(upper, halves[:, 0], halves[:, 1]).astype(wire)
        keep = jnp.where(upper, halves[:, 1], halves[:, 0])
        got = swap_bit(send, size, bit)
        held = keep + got.astype(F32)
    return held[0]


def row_major(values):
    return with_layout_constraint(values, Layout(tuple(range(values.ndim))))


def sinusoid(steps_given, width):
    half = width // 2
    freqs = jnp.exp(-math.log(10000.0) * jnp.arange(half, dtype=F32) / half)
    angles = steps_given.astype(F32)[..., None] * freqs
    return jnp.concatenate([jnp.sin(angles), jnp.cos(angles)], axis=-1)


def norm_parts(values):
    center = values - jnp.mean(values, axis=-1, keepdims=True)
    rate = lax.rsqrt(jnp.mean(center * center, axis=-1, keepdims=True) + epsilon)
    return center * rate, rate


def norm_pull(grad, xhat, rate, gain):
    c = grad * gain
    return rate * (
        c - jnp.mean(c, axis=-1, keepdims=True) - xhat * jnp.mean(c * xhat, axis=-1, keepdims=True)
    )


def gelu_both(values):
    cdf = 0.5 * (1.0 + lax.erf(values * math.sqrt(0.5)))
    slope = cdf + values * (jnp.exp(-0.5 * values * values) * (1.0 / math.sqrt(2.0 * math.pi)))
    return (values * cdf).astype(LOW), slope.astype(LOW)


def rows_dot(left, right):
    return dot32(left, right, (((0,), (0,)), ((), ())))


def column_sums(values):
    return rows_dot(jnp.ones((values.shape[0], 8), LOW), values)[0]


def take_half(values, which, axis):
    size = values.shape[axis] // 2
    return lax.dynamic_slice_in_dim(values, which * size, size, axis)


def layer(
    tokens, timesteps, lengths, time_weight, attn_gain, attn_shift, qkv_weight, out_weight,
    out_bias, mlp_gain, mlp_shift, up_weight, up_bias, down_weight, down_bias, cotangent, *, size
):
    local = tokens.shape[1]
    width = tokens.shape[2]
    half = width // 2
    wide = up_weight.shape[1]
    shard = time_weight.shape[0]
    deep = down_weight.shape[0]
    spot = lax.axis_index("seq")
    row = lax.axis_index("dp")
    chip = spot // 2
    core = spot % 2
    on_one = core == 1
    on_chip_one = chip == 1

    def natural(own, other, axis):
        return jnp.where(
            on_one,
            jnp.concatenate([other, own], axis=axis),
            jnp.concatenate([own, other], axis=axis),
        )

    pieces = [qkv_weight[:, k * half : (k + 1) * half] for k in range(6)]
    qkv_shard = jnp.where(
        on_one, jnp.concatenate(pieces[1::2], axis=1), jnp.concatenate(pieces[0::2], axis=1)
    ).astype(LOW)
    vectors = jnp.concatenate(
        [attn_gain, attn_shift, out_bias, mlp_gain, mlp_shift, down_bias, up_bias]
    ).astype(LOW).astype(F32)
    vectors = jnp.concatenate([timesteps.astype(F32), vectors])[None]
    qkv_shard, vectors, tokens, time_weight, up_weight, down_weight, out_weight = (
        lax.optimization_barrier(
            (qkv_shard, vectors, tokens, time_weight, up_weight, down_weight, out_weight)
        )
    )

    up_pairs = up_weight.astype(LOW).reshape(shard, size, 2, deep // 2)
    up_shard = lax.dynamic_index_in_dim(up_pairs, core, 2, False).reshape(shard, wide // 2)
    down_shard = take_half(down_weight.astype(LOW), core, 0)
    out_shard = take_half(out_weight.astype(LOW), core, 1)
    packed = jnp.concatenate(
        [
            up_shard[:, :width],
            up_shard[:, width:],
            down_shard,
            jnp.concatenate([out_shard[: shard // 2], out_shard[shard // 2 :]], axis=1),
        ],
        axis=0,
    )
    held = qkv_shard[None]
    for bit in reversed(bits_of(size)):
        if bit == 1:
            held, packed = lax.optimization_barrier((held, packed))
        held = gather_step(held, size, bit)
    qkv_own = held.reshape(width, 3 * half)
    own_pack = lax.all_gather(packed, "dp", axis=0, tiled=False)

    def unpack(pack):
        a = pack[:, :shard].reshape(width, width)
        b = pack[:, shard : 2 * shard].reshape(width, width)
        up = jnp.concatenate([a, b], axis=1)
        down = pack[:, 2 * shard : 2 * shard + deep // 2].reshape(wide // 2, width)
        return up, down

    def unpack_out(last):
        return jnp.concatenate([last[:, :, :half], last[:, :, half:]], axis=1).reshape(width, half)

    mine = lax.dynamic_index_in_dim(tokens, chip, 0, False)
    there = lax.dynamic_index_in_dim(tokens, 1 - chip, 0, False)
    source = jnp.concatenate([mine, swap_chip(there)], axis=0)
    small = gather_dp(vectors, size)[:, 0]
    steps = small[:, :2]
    gain_a, shift_a, bias_out, gain_m, shift_m, bias_down = [
        small[:, 2 + k * shard : 2 + (k + 1) * shard].reshape(width) for k in range(6)
    ]
    bias_up = small[:, 2 + 6 * shard :].reshape(size, 2, deep // 2)
    embedded = sinusoid(steps, width).astype(LOW)
    embedded = jnp.where(chip == 1, embedded[:, ::-1], embedded)
    own_rows = lax.dynamic_slice_in_dim(embedded, row * shard, shard, 2)
    time_parts = jnp.dot(own_rows[:, 0], time_weight.astype(LOW), preferred_element_type=F32)
    time_shift = scatter_dp(time_parts[:, None], size, F32)

    length = lax.dynamic_index_in_dim(lengths, chip, 0, False)
    places = jnp.arange(local, dtype=jnp.int32)

    def positions(which):
        return jnp.concatenate(
            [(2 * chip + which) * local + places, (2 * (1 - chip) + which) * local + places]
        )

    own_places = positions(core)
    valid = (own_places < length)[:, None]
    bias = jnp.where(
        jnp.concatenate([own_places, positions(1 - core)]) < length, 0.0, -1e30
    ).astype(F32)[:, None]

    hidden = row_major(row_major(source) + time_shift)
    xhat_a, rate_a = norm_parts(hidden)
    normed_own = (xhat_a * gain_a + shift_a).astype(LOW)
    normed_all = jnp.concatenate([normed_own, swap_core(normed_own)], axis=0)
    projected = jnp.dot(normed_all, qkv_own, preferred_element_type=F32).astype(LOW)
    projected, cotangent = lax.optimization_barrier((projected, cotangent))
    count = hidden.shape[0]
    lead = half // PAIR - 1
    mixed_one, wide_one, logs_one = attention_forward(projected, bias, 0, lead)
    mixed_one, own_pack, projected_late = lax.optimization_barrier((mixed_one, own_pack, projected))
    rest = 2 * shard + deep // 2
    other_out = swap_core(own_pack[:, rest:])
    other_pack = swap_core(own_pack[:, :rest])
    sent_one = swap_core(mixed_one[count:])
    mixed_two, wide_two, logs_two = attention_forward(projected_late, bias, lead, 1)
    attended = natural(
        jnp.concatenate([mixed_one[:count], mixed_two[:count]], axis=1),
        jnp.concatenate([sent_one, swap_core(mixed_two[count:])], axis=1),
        1,
    )
    wide_mixed = jnp.concatenate([wide_one, wide_two], axis=0)
    logs = jnp.concatenate([logs_one, logs_two], axis=0)

    cot_mine = lax.dynamic_index_in_dim(cotangent, chip, 0, False)
    cot_send = lax.dynamic_index_in_dim(cotangent, 1 - chip, 0, False)
    cot = jnp.concatenate([cot_mine, swap_chip(cot_send)], axis=0)
    cot = row_major(cot)
    out_full = natural(unpack_out(own_pack[:, rest:]), unpack_out(other_out), 1)
    up_a, down_a = unpack(own_pack)
    up_b, down_b = unpack(other_pack)
    bias_up_a = lax.dynamic_index_in_dim(bias_up, core, 1, False).reshape(wide // 2)
    bias_up_b = lax.dynamic_index_in_dim(bias_up, 1 - core, 1, False).reshape(wide // 2)

    middle = hidden + jnp.dot(attended, out_full, preferred_element_type=F32) + bias_out
    middle = row_major(middle)
    xhat_m, rate_m = norm_parts(middle)
    normed_two = (xhat_m * gain_m + shift_m).astype(LOW)
    act_a, slope_a = gelu_both(jnp.dot(normed_two, up_a, preferred_element_type=F32) + bias_up_a)
    act_b, slope_b = gelu_both(jnp.dot(normed_two, up_b, preferred_element_type=F32) + bias_up_b)
    branch = (
        jnp.dot(act_a, down_a, preferred_element_type=F32)
        + jnp.dot(act_b, down_b, preferred_element_type=F32)
        + bias_down
    )
    result = row_major(jnp.where(valid, middle + branch, 0.0))
    result_got = swap_chip(result[local:])

    grad_out = jnp.where(valid, cot, 0.0)
    grad_low = grad_out.astype(LOW)
    pre_a = (dot32(grad_low, down_a, NT) * slope_a.astype(F32)).astype(LOW)
    pre_b = (dot32(grad_low, down_b, NT) * slope_b.astype(F32)).astype(LOW)
    pre_a, pre_b = lax.optimization_barrier((pre_a, pre_b))
    grad_normed_two = row_major(dot32(pre_a, up_a, NT) + dot32(pre_b, up_b, NT))
    grad_middle = row_major(grad_out + norm_pull(grad_normed_two, xhat_m, rate_m, gain_m))
    grad_branch = grad_middle.astype(LOW)
    grad_attended = dot32(grad_branch, out_full, NT).astype(LOW)
    low_half, high_half = grad_attended[:, :half], grad_attended[:, half:]
    heads_own = jnp.where(on_one, high_half, low_half)
    heads_other = swap_core(jnp.where(on_one, low_half, high_half))
    grad_heads = jnp.concatenate([heads_own, heads_other], axis=0)

    def pack_grads(up, down, out):
        parts = [
            up[:, :width].reshape(size, shard, width),
            up[:, width:].reshape(size, shard, width),
            down.reshape(size, deep // 2, width),
        ]
        last = out.reshape(size, shard, half)
        parts.append(jnp.concatenate([last[:, : shard // 2], last[:, shard // 2 :]], axis=2))
        return jnp.concatenate([part.astype(LOW) for part in parts], axis=1)

    out_grad = rows_dot(attended, grad_branch)
    out_low, out_high = out_grad[:, :half], out_grad[:, half:]
    grads_a = pack_grads(
        rows_dot(normed_two, pre_a), rows_dot(act_a, grad_low), jnp.where(on_one, out_high, out_low)
    )
    grads_b = pack_grads(
        rows_dot(normed_two, pre_b), rows_dot(act_b, grad_low), jnp.where(on_one, out_low, out_high)
    )
    summed = (grads_a.astype(F32) + swap_core(grads_b).astype(F32)).astype(LOW)
    grad_heads, summed = lax.optimization_barrier((grad_heads, summed))
    shards = lax.psum_scatter(summed, "dp", scatter_dimension=0, tiled=False)
    dq, dk, dv = attention_backward(projected, wide_mixed, grad_heads, logs, bias, 0)
    grad_projected = jnp.concatenate([dq, dk, dv], axis=1)
    part_other = swap_core(dot32(grad_projected[count:], qkv_own, NT).astype(LOW))
    qkv_grad = rows_dot(normed_all, grad_projected).reshape(size, shard, 3 * half)
    (
        qkv_grad, grad_projected, pre_a, pre_b, grad_branch, grad_low, grad_normed_two,
    ) = lax.optimization_barrier(
        (qkv_grad, grad_projected, pre_a, pre_b, grad_branch, grad_low, grad_normed_two)
    )
    qkv_mine = scatter_dp(qkv_grad, size, LOW)
    qkv_mine = qkv_mine + swap_chip(qkv_mine.astype(LOW)).astype(F32)
    qkv_other = swap_core(qkv_mine)
    qkv_out = jnp.concatenate(
        [
            natural(
                qkv_mine[:, k * half : (k + 1) * half], qkv_other[:, k * half : (k + 1) * half], 1
            )
            for k in range(3)
        ],
        axis=1,
    )

    part_own = dot32(grad_projected[:count], qkv_own, NT)
    grad_normed_one = row_major(part_own + part_other.astype(F32))
    tokens_grad = row_major(
        grad_middle + norm_pull(grad_normed_one, xhat_a, rate_a, gain_a)
    )

    sum_bias_up = natural(
        column_sums(pre_a).reshape(size, 1, deep // 2),
        column_sums(pre_b).reshape(size, 1, deep // 2),
        1,
    ).reshape(size, deep)
    vector_sums = jnp.concatenate(
        [
            jnp.sum(grad_normed_one * xhat_a, axis=0).reshape(size, shard),
            jnp.sum(grad_normed_one, axis=0).reshape(size, shard),
            column_sums(grad_branch).reshape(size, shard),
            jnp.sum(grad_normed_two * xhat_m, axis=0).reshape(size, shard),
            jnp.sum(grad_normed_two, axis=0).reshape(size, shard),
            column_sums(grad_low).reshape(size, shard),
            sum_bias_up,
        ],
        axis=1,
    )
    token_sum = jnp.sum(tokens_grad, axis=0, keepdims=True)
    sums = jnp.concatenate([vector_sums.reshape(1, -1), token_sum], axis=1)
    sums = sums + swap_core(sums)
    sums_there = swap_chip(sums)
    tokens_grad, sums_there, result_got, result = lax.optimization_barrier(
        (tokens_grad, sums_there, result_got, result)
    )
    tokens_got = swap_chip(tokens_grad[local:].astype(LOW)).astype(F32)
    vector_sums = (sums + sums_there)[:, : vector_sums.size].reshape(vector_sums.shape)
    vector_mine = scatter_dp(vector_sums[:, None], size, F32)[0]
    vector_out = [vector_mine[k * shard : (k + 1) * shard] for k in range(6)]
    both = jnp.concatenate([sums, sums_there], axis=0)[:, -width:]
    gathered = gather_dp(both, size)
    sums_own = gathered[:, 0]
    sums_other = gathered[:, 1]
    exact = dict(precision=lax.Precision.HIGHEST, preferred_element_type=F32)
    contract = (((0,), (0,)), ((), ()))
    time_grad = lax.dot_general(
        own_rows[:, 0].astype(F32), sums_own, contract, **exact
    ) + lax.dot_general(own_rows[:, 1].astype(F32), sums_other, contract, **exact)

    shards = shards.astype(F32)
    shards = shards + swap_chip(shards.astype(LOW)).astype(F32)
    shards_other = swap_core(shards.astype(LOW)).astype(F32)

    def unpack_grads(pack):
        up = jnp.concatenate([pack[:shard], pack[shard : 2 * shard]], axis=1)
        down = pack[2 * shard : 2 * shard + deep // 2]
        last = pack[2 * shard + deep // 2 :]
        return up, down, jnp.concatenate([last[:, :half], last[:, half:]], axis=0)

    up_ga, down_ga, out_ga = unpack_grads(shards)
    up_gb, down_gb, out_gb = unpack_grads(shards_other)
    up_out = natural(
        up_ga.reshape(shard, size, 1, deep // 2), up_gb.reshape(shard, size, 1, deep // 2), 2
    ).reshape(shard, wide)

    def hand_back(kept, got):
        return row_major(
            jnp.where(on_chip_one, jnp.stack([got, kept]), jnp.stack([kept, got]))
        )

    return (
        hand_back(result[:local], result_got),
        hand_back(tokens_grad[:local], tokens_got),
        time_grad,
        vector_out[0],
        vector_out[1],
        qkv_out,
        natural(out_ga, out_gb, 1),
        vector_out[2],
        vector_out[3],
        vector_out[4],
        up_out,
        vector_mine[6 * shard :],
        natural(down_ga, down_gb, 0),
        vector_out[5],
    )


def solution(mesh):
    batch = P("dp", "seq", None)
    flat = P("dp")
    grid = P("dp", None)
    in_specs = (
        batch, flat, flat, grid, flat, flat, grid, grid, flat, flat, flat, grid, flat, grid, flat,
        batch,
    )
    out_specs = (
        batch, batch, grid, flat, flat, grid, grid, flat, flat, flat, grid, flat, grid, flat,
    )
    body = functools.partial(layer, size=mesh.shape["dp"])
    return jax.shard_map(
        body, mesh=mesh, in_specs=in_specs, out_specs=out_specs, check_vma=False
    )
```

```python
import functools, math
import jax, jax.numpy as jnp
from jax import lax
from jax.experimental import pallas as pl
from jax.experimental.layout import Layout, with_layout_constraint
from jax.experimental.pallas import tpu as pltpu
from jax.sharding import PartitionSpec as P


HEAD = 64
PAIR = 2 * HEAD
NT = (((1,), (1,)), ((), ()))
NN = (((1,), (0,)), ((), ()))
SCALE = 1.0 / math.sqrt(HEAD)


def dot32(left, right, dims):
    return lax.dot_general(left, right, dims, preferred_element_type=jnp.float32)


def one_head(block, which):
    lane = lax.broadcasted_iota(jnp.int32, block.shape, 1)
    return jnp.where(lane // HEAD == which, block.astype(jnp.float32), 0.0)


def attention_forward_kernel(bias_ref, q_ref, k_ref, v_ref, out_ref, wide_ref, log_ref, vt_ref, *, chunk):
    @pl.when(pl.program_id(1) == 0)
    def _():
        vt_ref[...] = v_ref[...].T

    total = k_ref.shape[0]
    mixed = []
    for which in range(2):
        query = (one_head(q_ref[...], which) * SCALE).astype(jnp.bfloat16)
        scores = []
        for start in range(0, total, chunk):
            rows = pl.ds(start, chunk)
            part = dot32(k_ref[rows, :], query, NT) + bias_ref[rows, :]
            scores.append(part)
        top = jnp.max(scores[0], axis=0, keepdims=True)
        for part in scores[1:]:
            top = jnp.maximum(top, jnp.max(part, axis=0, keepdims=True))
        totals = 0.0
        acc = 0.0
        for index, part in enumerate(scores):
            weights = jnp.exp(part - top)
            totals = totals + jnp.sum(weights, axis=0, keepdims=True)
            values = vt_ref[which * HEAD : (which + 1) * HEAD, index * chunk : (index + 1) * chunk]
            acc = acc + dot32(values, weights.astype(jnp.bfloat16), NN)
        mixed.append(acc / totals)
        log_ref[0, which : which + 1, :] = top + jnp.log(totals)
    joined = jnp.concatenate(mixed, axis=0)
    wide_ref[0] = joined
    out_ref[...] = joined.T.astype(jnp.bfloat16)


def attention_backward_kernel(
    bias_ref, q_ref, k_ref, v_ref, mixed_ref, grad_ref, log_ref,
    dq_ref, dk_ref, dv_ref, kt_ref, dk_acc, dv_acc, *, chunk
):
    step = pl.program_id(1)

    @pl.when(step == 0)
    def _():
        kt_ref[...] = k_ref[...].T
        dk_acc[...] = jnp.zeros_like(dk_acc)
        dv_acc[...] = jnp.zeros_like(dv_acc)

    total = k_ref.shape[0]
    centre_t = grad_ref[...].astype(jnp.float32).T * mixed_ref[0]
    queries = []
    grads = []
    for which in range(2):
        queries.append((one_head(q_ref[...], which) * SCALE).astype(jnp.bfloat16))
        grads.append(one_head(grad_ref[...], which).astype(jnp.bfloat16))
    dq_parts = [0.0, 0.0]
    for start in range(0, total, chunk):
        rows = pl.ds(start, chunk)
        dk_part = dk_acc[rows, :]
        dv_part = dv_acc[rows, :]
        for which in range(2):
            head = slice(which * HEAD, (which + 1) * HEAD)
            centre = jnp.sum(centre_t[head, :], axis=0, keepdims=True)
            scores = dot32(k_ref[rows, :], queries[which], NT) + bias_ref[rows, :]
            probs = jnp.exp(scores - log_ref[0, which : which + 1, :])
            grad_probs = dot32(v_ref[rows, :], grads[which], NT)
            grad_scores = (probs * (grad_probs - centre)).astype(jnp.bfloat16)
            dv_part = dv_part + dot32(probs.astype(jnp.bfloat16), grads[which], NN)
            dk_part = dk_part + dot32(grad_scores, queries[which], NN)
            dq_parts[which] = dq_parts[which] + dot32(
                kt_ref[head, start : start + chunk], grad_scores, NN
            )
        dk_acc[rows, :] = dk_part
        dv_acc[rows, :] = dv_part
    dq_ref[...] = (jnp.concatenate(dq_parts, axis=0).T * SCALE).astype(jnp.bfloat16)

    @pl.when(step == pl.num_programs(1) - 1)
    def _():
        dk_ref[...] = dk_acc[...].astype(jnp.bfloat16)
        dv_ref[...] = dv_acc[...].astype(jnp.bfloat16)


def cost_of(total, pairs, products):
    return pl.CostEstimate(
        flops=pairs * 2 * products * 2 * total * total * 4 * HEAD,
        transcendentals=pairs * 2 * total * total,
        bytes_accessed=pairs * total * PAIR * 16,
    )


def attention_forward(projected, bias, first, pairs, block=512, chunk=512):
    total = projected.shape[0]
    every = projected.shape[1] // (3 * PAIR)
    block = min(block, total)
    return pl.pallas_call(
        functools.partial(attention_forward_kernel, chunk=min(chunk, total)),
        name="attention_forward",
        cost_estimate=cost_of(total, pairs, 2),
        grid=(pairs, total // block),
        in_specs=[
            pl.BlockSpec((total, 1), lambda p, i: (0, 0)),
            pl.BlockSpec((block, PAIR), lambda p, i: (i, first + p)),
            pl.BlockSpec((total, PAIR), lambda p, i: (0, every + first + p)),
            pl.BlockSpec((total, PAIR), lambda p, i: (0, 2 * every + first + p)),
        ],
        out_specs=[
            pl.BlockSpec((block, PAIR), lambda p, i: (i, p)),
            pl.BlockSpec((1, PAIR, block), lambda p, i: (p, 0, i)),
            pl.BlockSpec((1, 2, block), lambda p, i: (p, 0, i)),
        ],
        out_shape=[
            jax.ShapeDtypeStruct((total, pairs * PAIR), jnp.bfloat16),
            jax.ShapeDtypeStruct((pairs, PAIR, total), jnp.float32),
            jax.ShapeDtypeStruct((pairs, 2, total), jnp.float32),
        ],
        scratch_shapes=[pltpu.VMEM((PAIR, total), jnp.bfloat16)],
    )(bias, projected, projected, projected)


def attention_backward(projected, mixed, grad_mixed, logs, bias, first, block=512, chunk=256):
    total = projected.shape[0]
    every = projected.shape[1] // (3 * PAIR)
    pairs = mixed.shape[0]
    block = min(block, total)
    out = jax.ShapeDtypeStruct((total, pairs * PAIR), jnp.bfloat16)
    return pl.pallas_call(
        functools.partial(attention_backward_kernel, chunk=min(chunk, total)),
        name="attention_backward",
        cost_estimate=cost_of(total, pairs, 5),
        grid=(pairs, total // block),
        in_specs=[
            pl.BlockSpec((total, 1), lambda p, i: (0, 0)),
            pl.BlockSpec((block, PAIR), lambda p, i: (i, first + p)),
            pl.BlockSpec((total, PAIR), lambda p, i: (0, every + first + p)),
            pl.BlockSpec((total, PAIR), lambda p, i: (0, 2 * every + first + p)),
            pl.BlockSpec((1, PAIR, block), lambda p, i: (p, 0, i)),
            pl.BlockSpec((block, PAIR), lambda p, i: (i, first + p)),
            pl.BlockSpec((1, 2, block), lambda p, i: (p, 0, i)),
        ],
        out_specs=[
            pl.BlockSpec((block, PAIR), lambda p, i: (i, p)),
            pl.BlockSpec((total, PAIR), lambda p, i: (0, p)),
            pl.BlockSpec((total, PAIR), lambda p, i: (0, p)),
        ],
        out_shape=[out, out, out],
        scratch_shapes=[
            pltpu.VMEM((PAIR, total), jnp.bfloat16),
            pltpu.VMEM((total, PAIR), jnp.float32),
            pltpu.VMEM((total, PAIR), jnp.float32),
        ],
    )(bias, projected, projected, projected, mixed, grad_mixed, logs)


epsilon = 1e-05

CORE_SWAP = ((0, 1), (1, 0), (2, 3), (3, 2))
CHIP_SWAP = ((0, 2), (2, 0), (1, 3), (3, 1))
LOW = jnp.bfloat16
F32 = jnp.float32


def swap_core(values):
    return lax.ppermute(values, "seq", CORE_SWAP)


def swap_chip(values):
    return lax.ppermute(values, "seq", CHIP_SWAP)


def swap_bit(values, size, bit):
    return lax.ppermute(values, "dp", [(i, i ^ bit) for i in range(size)])


def bits_of(size):
    return [1 << b for b in range(size.bit_length() - 1)]


def gather_step(held, size, bit):
    upper = (lax.axis_index("dp") & bit) != 0
    got = swap_bit(held, size, bit)
    first = jnp.where(upper, got, held)
    second = jnp.where(upper, held, got)
    return jnp.stack([first, second], axis=1).reshape((-1,) + held.shape[1:])


def gather_dp(values, size):
    held = values[None]
    for bit in bits_of(size):
        upper = (lax.axis_index("dp") & bit) != 0
        got = swap_bit(held, size, bit)
        held = jnp.concatenate([jnp.where(upper, got, held), jnp.where(upper, held, got)], axis=0)
    return held


def scatter_dp(values, size, wire, gate=()):
    me = lax.axis_index("dp")
    held = values
    for bit in bits_of(size):
        upper = (me & bit) != 0
        halves = held.reshape((held.shape[0] // 2, 2) + held.shape[1:])
        send = jnp.where(upper, halves[:, 0], halves[:, 1]).astype(wire)
        keep = jnp.where(upper, halves[:, 1], halves[:, 0])
        if bit == 1 and gate:
            send, *gate = lax.optimization_barrier((send, *gate))
        got = swap_bit(send, size, bit)
        held = keep + got.astype(F32)
    return (held[0], *gate) if gate else held[0]


def row_major(values):
    return with_layout_constraint(values, Layout(tuple(range(values.ndim))))


def sinusoid(steps_given, width):
    half = width // 2
    freqs = jnp.exp(-math.log(10000.0) * jnp.arange(half, dtype=F32) / half)
    angles = steps_given.astype(F32)[..., None] * freqs
    return jnp.concatenate([jnp.sin(angles), jnp.cos(angles)], axis=-1)


def norm_parts(values):
    center = values - jnp.mean(values, axis=-1, keepdims=True)
    rate = lax.rsqrt(jnp.mean(center * center, axis=-1, keepdims=True) + epsilon)
    return center * rate, rate


def norm_pull(grad, xhat, rate, gain):
    c = grad * gain
    return rate * (
        c - jnp.mean(c, axis=-1, keepdims=True) - xhat * jnp.mean(c * xhat, axis=-1, keepdims=True)
    )


def gelu_both(values):
    cdf = 0.5 * (1.0 + lax.erf(values * math.sqrt(0.5)))
    slope = cdf + values * (jnp.exp(-0.5 * values * values) * (1.0 / math.sqrt(2.0 * math.pi)))
    return (values * cdf).astype(LOW), slope.astype(LOW)


def rows_dot(left, right):
    return dot32(left, right, (((0,), (0,)), ((), ())))


def column_sums(values):
    return rows_dot(jnp.ones((values.shape[0], 8), LOW), values)[0]


def take_half(values, which, axis):
    size = values.shape[axis] // 2
    return lax.dynamic_slice_in_dim(values, which * size, size, axis)


def layer(
    tokens, timesteps, lengths, time_weight, attn_gain, attn_shift, qkv_weight, out_weight,
    out_bias, mlp_gain, mlp_shift, up_weight, up_bias, down_weight, down_bias, cotangent, *, size
):
    local = tokens.shape[1]
    width = tokens.shape[2]
    half = width // 2
    wide = up_weight.shape[1]
    shard = time_weight.shape[0]
    deep = down_weight.shape[0]
    spot = lax.axis_index("seq")
    row = lax.axis_index("dp")
    chip = spot // 2
    core = spot % 2
    on_one = core == 1
    on_chip_one = chip == 1

    def natural(own, other, axis):
        return jnp.where(
            on_one,
            jnp.concatenate([other, own], axis=axis),
            jnp.concatenate([own, other], axis=axis),
        )

    pieces = [qkv_weight[:, k * half : (k + 1) * half] for k in range(6)]
    qkv_shard = jnp.where(
        on_one, jnp.concatenate(pieces[1::2], axis=1), jnp.concatenate(pieces[0::2], axis=1)
    ).astype(LOW)
    vectors = jnp.concatenate(
        [attn_gain, attn_shift, out_bias, mlp_gain, mlp_shift, down_bias, up_bias]
    ).astype(LOW).astype(F32)
    vectors = jnp.concatenate([timesteps.astype(F32), vectors])[None]
    qkv_shard, vectors, tokens, time_weight, up_weight, down_weight, out_weight = (
        lax.optimization_barrier(
            (qkv_shard, vectors, tokens, time_weight, up_weight, down_weight, out_weight)
        )
    )

    def pack_weights(up_weight, down_weight, out_weight):
        up_pairs = up_weight.astype(LOW).reshape(shard, size, 2, deep // 2)
        up_shard = lax.dynamic_index_in_dim(up_pairs, core, 2, False).reshape(shard, wide // 2)
        down_shard = take_half(down_weight.astype(LOW), core, 0)
        out_shard = take_half(out_weight.astype(LOW), core, 1)
        return jnp.concatenate(
            [
                up_shard[:, :width],
                up_shard[:, width:],
                down_shard,
                jnp.concatenate([out_shard[: shard // 2], out_shard[shard // 2 :]], axis=1),
            ],
            axis=0,
        )

    held = qkv_shard[None]
    for bit in reversed(bits_of(size)):
        if bit == 2:
            held, up_weight, down_weight, out_weight = lax.optimization_barrier(
                (held, up_weight, down_weight, out_weight)
            )
        if bit == 1:
            held, packed = lax.optimization_barrier(
                (held, pack_weights(up_weight, down_weight, out_weight))
            )
        held = gather_step(held, size, bit)
    qkv_own = held.reshape(width, 3 * half)
    own_pack = lax.all_gather(packed, "dp", axis=0, tiled=False)

    def unpack(pack):
        a = pack[:, :shard].reshape(width, width)
        b = pack[:, shard : 2 * shard].reshape(width, width)
        up = jnp.concatenate([a, b], axis=1)
        down = pack[:, 2 * shard : 2 * shard + deep // 2].reshape(wide // 2, width)
        return up, down

    def unpack_out(last):
        return jnp.concatenate([last[:, :, :half], last[:, :, half:]], axis=1).reshape(width, half)

    mine = lax.dynamic_index_in_dim(tokens, chip, 0, False)
    there = lax.dynamic_index_in_dim(tokens, 1 - chip, 0, False)
    source = jnp.concatenate([mine, swap_chip(there)], axis=0)
    small = gather_dp(vectors, size)[:, 0]
    steps = small[:, :2]
    gain_a, shift_a, bias_out, gain_m, shift_m, bias_down = [
        small[:, 2 + k * shard : 2 + (k + 1) * shard].reshape(width) for k in range(6)
    ]
    bias_up = small[:, 2 + 6 * shard :].reshape(size, 2, deep // 2)
    embedded = sinusoid(steps, width).astype(LOW)
    embedded = jnp.where(chip == 1, embedded[:, ::-1], embedded)
    own_rows = lax.dynamic_slice_in_dim(embedded, row * shard, shard, 2)
    time_parts = jnp.dot(own_rows[:, 0], time_weight.astype(LOW), preferred_element_type=F32)
    time_shift = scatter_dp(time_parts[:, None], size, F32)

    length = lax.dynamic_index_in_dim(lengths, chip, 0, False)
    places = jnp.arange(local, dtype=jnp.int32)

    def positions(which):
        return jnp.concatenate(
            [(2 * chip + which) * local + places, (2 * (1 - chip) + which) * local + places]
        )

    own_places = positions(core)
    valid = (own_places < length)[:, None]
    bias = jnp.where(
        jnp.concatenate([own_places, positions(1 - core)]) < length, 0.0, -1e30
    ).astype(F32)[:, None]

    hidden = row_major(row_major(source) + time_shift)
    xhat_a, rate_a = norm_parts(hidden)
    normed_own = (xhat_a * gain_a + shift_a).astype(LOW)
    normed_all = jnp.concatenate([normed_own, swap_core(normed_own)], axis=0)
    projected = jnp.dot(normed_all, qkv_own, preferred_element_type=F32).astype(LOW)
    projected, cotangent = lax.optimization_barrier((projected, cotangent))
    count = hidden.shape[0]
    lead = half // PAIR - 1
    mixed_one, wide_one, logs_one = attention_forward(projected, bias, 0, lead)
    mixed_one, own_pack, projected_late = lax.optimization_barrier((mixed_one, own_pack, projected))
    rest = 2 * shard + deep // 2
    other_out = swap_core(own_pack[:, rest:])
    other_pack = swap_core(own_pack)
    sent_one = swap_core(mixed_one[count:])
    mixed_two, wide_two, logs_two = attention_forward(projected_late, bias, lead, 1)
    attended = natural(
        jnp.concatenate([mixed_one[:count], mixed_two[:count]], axis=1),
        jnp.concatenate([sent_one, swap_core(mixed_two[count:])], axis=1),
        1,
    )

    cot_mine = lax.dynamic_index_in_dim(cotangent, chip, 0, False)
    cot_send = lax.dynamic_index_in_dim(cotangent, 1 - chip, 0, False)
    cot = jnp.concatenate([cot_mine, swap_chip(cot_send)], axis=0)
    cot = row_major(cot)
    out_full = natural(unpack_out(own_pack[:, rest:]), unpack_out(other_out), 1)
    up_a, down_a = unpack(own_pack)
    up_b, down_b = unpack(other_pack)
    bias_up_a = lax.dynamic_index_in_dim(bias_up, core, 1, False).reshape(wide // 2)
    bias_up_b = lax.dynamic_index_in_dim(bias_up, 1 - core, 1, False).reshape(wide // 2)

    middle = hidden + jnp.dot(attended, out_full, preferred_element_type=F32) + bias_out
    middle = row_major(middle)
    xhat_m, rate_m = norm_parts(middle)
    normed_two = (xhat_m * gain_m + shift_m).astype(LOW)
    act_a, slope_a = gelu_both(jnp.dot(normed_two, up_a, preferred_element_type=F32) + bias_up_a)
    act_b, slope_b = gelu_both(jnp.dot(normed_two, up_b, preferred_element_type=F32) + bias_up_b)
    branch = (
        jnp.dot(act_a, down_a, preferred_element_type=F32)
        + jnp.dot(act_b, down_b, preferred_element_type=F32)
        + bias_down
    )
    result = row_major(jnp.where(valid, middle + branch, 0.0))
    result_got = swap_chip(result[local:])

    grad_out = jnp.where(valid, cot, 0.0)
    grad_low = grad_out.astype(LOW)
    pre_a = (dot32(grad_low, down_a, NT) * slope_a.astype(F32)).astype(LOW)
    pre_b = (dot32(grad_low, down_b, NT) * slope_b.astype(F32)).astype(LOW)
    pre_a, pre_b = lax.optimization_barrier((pre_a, pre_b))
    grad_normed_two = row_major(dot32(pre_a, up_a, NT) + dot32(pre_b, up_b, NT))
    grad_middle = row_major(grad_out + norm_pull(grad_normed_two, xhat_m, rate_m, gain_m))
    grad_branch = grad_middle.astype(LOW)
    grad_attended = dot32(grad_branch, out_full, NT).astype(LOW)
    low_half, high_half = grad_attended[:, :half], grad_attended[:, half:]
    heads_own = jnp.where(on_one, high_half, low_half)
    heads_other = swap_core(jnp.where(on_one, low_half, high_half))
    grad_heads = jnp.concatenate([heads_own, heads_other], axis=0)

    def pack_grads(up, down, out):
        parts = [
            up[:, :width].reshape(size, shard, width),
            up[:, width:].reshape(size, shard, width),
            down.reshape(size, deep // 2, width),
        ]
        last = out.reshape(size, shard, half)
        parts.append(jnp.concatenate([last[:, : shard // 2], last[:, shard // 2 :]], axis=2))
        return jnp.concatenate([part.astype(LOW) for part in parts], axis=1)

    out_grad = rows_dot(attended, grad_branch)
    out_low, out_high = out_grad[:, :half], out_grad[:, half:]
    grads_a = pack_grads(
        rows_dot(normed_two, pre_a), rows_dot(act_a, grad_low), jnp.where(on_one, out_high, out_low)
    )
    grads_b = pack_grads(
        rows_dot(normed_two, pre_b), rows_dot(act_b, grad_low), jnp.where(on_one, out_low, out_high)
    )
    summed = (grads_a.astype(F32) + swap_core(grads_b).astype(F32)).astype(LOW)
    grad_heads, summed = lax.optimization_barrier((grad_heads, summed))
    shards = lax.psum_scatter(summed, "dp", scatter_dimension=0, tiled=False)
    cut = lead * PAIR
    grad_a = jnp.concatenate(
        attention_backward(projected, wide_one, grad_heads, logs_one, bias, 0), axis=1
    )
    qkv_a = rows_dot(normed_all, grad_a).reshape(size, 2, shard // 2, 3 * cut)
    qkv_keep = jnp.where(on_chip_one, qkv_a[:, 1], qkv_a[:, 0])
    qkv_send = jnp.where(on_chip_one, qkv_a[:, 0], qkv_a[:, 1]).astype(LOW)
    qkv_got = swap_chip(qkv_send)
    grad_b = jnp.concatenate(
        attention_backward(projected, wide_two, grad_heads, logs_two, bias, lead), axis=1
    )
    columns = [qkv_own[:, k * half : (k + 1) * half] for k in range(3)]
    weight_a = jnp.concatenate([part[:, :cut] for part in columns], axis=1)
    weight_b = jnp.concatenate([part[:, cut:] for part in columns], axis=1)
    part_other = dot32(grad_a[count:], weight_a, NT) + dot32(grad_b[count:], weight_b, NT)
    part_other = swap_core(part_other.astype(LOW))
    qkv_b = rows_dot(normed_all, grad_b).reshape(size, shard, 3 * (half - cut))
    qkv_b, grad_a, grad_b, pre_a, pre_b, grad_branch, grad_low, grad_normed_two = scatter_dp(
        qkv_b, size, LOW, (grad_a, grad_b, pre_a, pre_b, grad_branch, grad_low, grad_normed_two)
    )
    qkv_a = scatter_dp(qkv_keep + qkv_got.astype(F32), size, LOW)
    qkv_more = swap_chip(qkv_a)
    qkv_a = jnp.where(
        on_chip_one,
        jnp.concatenate([qkv_more, qkv_a], axis=0),
        jnp.concatenate([qkv_a, qkv_more], axis=0),
    )
    qkv_b = qkv_b + swap_chip(qkv_b.astype(LOW)).astype(F32)
    qkv_mine = jnp.concatenate(
        [
            piece
            for k in range(3)
            for piece in (
                qkv_a[:, k * cut : (k + 1) * cut],
                qkv_b[:, k * (half - cut) : (k + 1) * (half - cut)],
            )
        ],
        axis=1,
    )
    qkv_other = swap_core(qkv_mine)
    qkv_out = jnp.concatenate(
        [
            natural(
                qkv_mine[:, k * half : (k + 1) * half], qkv_other[:, k * half : (k + 1) * half], 1
            )
            for k in range(3)
        ],
        axis=1,
    )

    part_own = dot32(grad_a[:count], weight_a, NT) + dot32(grad_b[:count], weight_b, NT)
    grad_normed_one = row_major(part_own + part_other.astype(F32))
    tokens_grad = row_major(
        grad_middle + norm_pull(grad_normed_one, xhat_a, rate_a, gain_a)
    )

    sum_bias_up = natural(
        column_sums(pre_a).reshape(size, 1, deep // 2),
        column_sums(pre_b).reshape(size, 1, deep // 2),
        1,
    ).reshape(size, deep)
    vector_sums = jnp.concatenate(
        [
            jnp.sum(grad_normed_one * xhat_a, axis=0).reshape(size, shard),
            jnp.sum(grad_normed_one, axis=0).reshape(size, shard),
            column_sums(grad_branch).reshape(size, shard),
            jnp.sum(grad_normed_two * xhat_m, axis=0).reshape(size, shard),
            jnp.sum(grad_normed_two, axis=0).reshape(size, shard),
            column_sums(grad_low).reshape(size, shard),
            sum_bias_up,
        ],
        axis=1,
    )
    token_sum = jnp.sum(tokens_grad, axis=0, keepdims=True)
    sums = jnp.concatenate([vector_sums.reshape(1, -1), token_sum], axis=1)
    sums = sums + swap_core(sums)
    sums_there = swap_chip(sums)
    sums_there, result_got, result = lax.optimization_barrier((sums_there, result_got, result))
    tokens_got = swap_chip(tokens_grad[local:].astype(LOW)).astype(F32)
    vector_sums = (sums + sums_there)[:, : vector_sums.size].reshape(vector_sums.shape)
    vector_mine = scatter_dp(vector_sums[:, None], size, F32)[0]
    vector_out = [vector_mine[k * shard : (k + 1) * shard] for k in range(6)]
    both = jnp.concatenate([sums, sums_there], axis=0)[:, -width:]
    gathered = gather_dp(both, size)
    sums_own = gathered[:, 0]
    sums_other = gathered[:, 1]
    exact = dict(precision=lax.Precision.HIGHEST, preferred_element_type=F32)
    contract = (((0,), (0,)), ((), ()))
    time_grad = lax.dot_general(
        own_rows[:, 0].astype(F32), sums_own, contract, **exact
    ) + lax.dot_general(own_rows[:, 1].astype(F32), sums_other, contract, **exact)

    shards = shards.astype(F32)
    shards = shards + swap_chip(shards.astype(LOW)).astype(F32)
    shards_other = swap_core(shards.astype(LOW)).astype(F32)

    def unpack_grads(pack):
        up = jnp.concatenate([pack[:shard], pack[shard : 2 * shard]], axis=1)
        down = pack[2 * shard : 2 * shard + deep // 2]
        last = pack[2 * shard + deep // 2 :]
        return up, down, jnp.concatenate([last[:, :half], last[:, half:]], axis=0)

    up_ga, down_ga, out_ga = unpack_grads(shards)
    up_gb, down_gb, out_gb = unpack_grads(shards_other)
    up_out = natural(
        up_ga.reshape(shard, size, 1, deep // 2), up_gb.reshape(shard, size, 1, deep // 2), 2
    ).reshape(shard, wide)

    def hand_back(kept, got):
        return row_major(
            jnp.where(on_chip_one, jnp.stack([got, kept]), jnp.stack([kept, got]))
        )

    return (
        hand_back(result[:local], result_got),
        hand_back(tokens_grad[:local], tokens_got),
        time_grad,
        vector_out[0],
        vector_out[1],
        qkv_out,
        natural(out_ga, out_gb, 1),
        vector_out[2],
        vector_out[3],
        vector_out[4],
        up_out,
        vector_mine[6 * shard :],
        natural(down_ga, down_gb, 0),
        vector_out[5],
    )


def solution(mesh):
    batch = P("dp", "seq", None)
    flat = P("dp")
    grid = P("dp", None)
    in_specs = (
        batch, flat, flat, grid, flat, flat, grid, grid, flat, flat, flat, grid, flat, grid, flat,
        batch,
    )
    out_specs = (
        batch, batch, grid, flat, flat, grid, grid, flat, flat, flat, grid, flat, grid, flat,
    )
    body = functools.partial(layer, size=mesh.shape["dp"])
    return jax.shard_map(
        body, mesh=mesh, in_specs=in_specs, out_specs=out_specs, check_vma=False
    )
```

```python
import functools, math
import jax, jax.numpy as jnp
from jax import lax
from jax.experimental import pallas as pl
from jax.experimental.layout import Layout, with_layout_constraint
from jax.experimental.pallas import tpu as pltpu
from jax.sharding import PartitionSpec as P


HEAD = 64
PAIR = 2 * HEAD
NT = (((1,), (1,)), ((), ()))
NN = (((1,), (0,)), ((), ()))
SCALE = 1.0 / math.sqrt(HEAD)


def dot32(left, right, dims):
    return lax.dot_general(left, right, dims, preferred_element_type=jnp.float32)


def one_head(block, which):
    lane = lax.broadcasted_iota(jnp.int32, block.shape, 1)
    return jnp.where(lane // HEAD == which, block.astype(jnp.float32), 0.0)


def attention_forward_kernel(bias_ref, q_ref, k_ref, v_ref, out_ref, wide_ref, log_ref, vt_ref, *, chunk):
    @pl.when(pl.program_id(1) == 0)
    def _():
        vt_ref[...] = v_ref[...].T

    total = k_ref.shape[0]
    mixed = []
    for which in range(2):
        query = (one_head(q_ref[...], which) * SCALE).astype(jnp.bfloat16)
        scores = []
        for start in range(0, total, chunk):
            rows = pl.ds(start, chunk)
            part = dot32(k_ref[rows, :], query, NT) + bias_ref[rows, :]
            scores.append(part)
        top = jnp.max(scores[0], axis=0, keepdims=True)
        for part in scores[1:]:
            top = jnp.maximum(top, jnp.max(part, axis=0, keepdims=True))
        totals = 0.0
        acc = 0.0
        for index, part in enumerate(scores):
            weights = jnp.exp(part - top)
            totals = totals + jnp.sum(weights, axis=0, keepdims=True)
            values = vt_ref[which * HEAD : (which + 1) * HEAD, index * chunk : (index + 1) * chunk]
            acc = acc + dot32(values, weights.astype(jnp.bfloat16), NN)
        mixed.append(acc / totals)
        log_ref[0, which : which + 1, :] = top + jnp.log(totals)
    joined = jnp.concatenate(mixed, axis=0)
    wide_ref[0] = joined
    out_ref[...] = joined.T.astype(jnp.bfloat16)


def attention_backward_kernel(
    bias_ref, q_ref, k_ref, v_ref, mixed_ref, grad_ref, log_ref,
    dq_ref, dk_ref, dv_ref, kt_ref, dk_acc, dv_acc, *, chunk
):
    step = pl.program_id(1)

    @pl.when(step == 0)
    def _():
        kt_ref[...] = k_ref[...].T
        dk_acc[...] = jnp.zeros_like(dk_acc)
        dv_acc[...] = jnp.zeros_like(dv_acc)

    total = k_ref.shape[0]
    centre_t = grad_ref[...].astype(jnp.float32).T * mixed_ref[0]
    queries = []
    grads = []
    for which in range(2):
        queries.append((one_head(q_ref[...], which) * SCALE).astype(jnp.bfloat16))
        grads.append(one_head(grad_ref[...], which).astype(jnp.bfloat16))
    dq_parts = [0.0, 0.0]
    for start in range(0, total, chunk):
        rows = pl.ds(start, chunk)
        dk_part = dk_acc[rows, :]
        dv_part = dv_acc[rows, :]
        for which in range(2):
            head = slice(which * HEAD, (which + 1) * HEAD)
            centre = jnp.sum(centre_t[head, :], axis=0, keepdims=True)
            scores = dot32(k_ref[rows, :], queries[which], NT) + bias_ref[rows, :]
            probs = jnp.exp(scores - log_ref[0, which : which + 1, :])
            grad_probs = dot32(v_ref[rows, :], grads[which], NT)
            grad_scores = (probs * (grad_probs - centre)).astype(jnp.bfloat16)
            dv_part = dv_part + dot32(probs.astype(jnp.bfloat16), grads[which], NN)
            dk_part = dk_part + dot32(grad_scores, queries[which], NN)
            dq_parts[which] = dq_parts[which] + dot32(
                kt_ref[head, start : start + chunk], grad_scores, NN
            )
        dk_acc[rows, :] = dk_part
        dv_acc[rows, :] = dv_part
    dq_ref[...] = (jnp.concatenate(dq_parts, axis=0).T * SCALE).astype(jnp.bfloat16)

    @pl.when(step == pl.num_programs(1) - 1)
    def _():
        dk_ref[...] = dk_acc[...].astype(jnp.bfloat16)
        dv_ref[...] = dv_acc[...].astype(jnp.bfloat16)


def cost_of(total, pairs, products):
    return pl.CostEstimate(
        flops=pairs * 2 * products * 2 * total * total * 4 * HEAD,
        transcendentals=pairs * 2 * total * total,
        bytes_accessed=pairs * total * PAIR * 16,
    )


def attention_forward(projected, bias, first, pairs, block=512, chunk=512):
    total = projected.shape[0]
    every = projected.shape[1] // (3 * PAIR)
    block = min(block, total)
    return pl.pallas_call(
        functools.partial(attention_forward_kernel, chunk=min(chunk, total)),
        name="attention_forward",
        cost_estimate=cost_of(total, pairs, 2),
        grid=(pairs, total // block),
        in_specs=[
            pl.BlockSpec((total, 1), lambda p, i: (0, 0)),
            pl.BlockSpec((block, PAIR), lambda p, i: (i, first + p)),
            pl.BlockSpec((total, PAIR), lambda p, i: (0, every + first + p)),
            pl.BlockSpec((total, PAIR), lambda p, i: (0, 2 * every + first + p)),
        ],
        out_specs=[
            pl.BlockSpec((block, PAIR), lambda p, i: (i, p)),
            pl.BlockSpec((1, PAIR, block), lambda p, i: (p, 0, i)),
            pl.BlockSpec((1, 2, block), lambda p, i: (p, 0, i)),
        ],
        out_shape=[
            jax.ShapeDtypeStruct((total, pairs * PAIR), jnp.bfloat16),
            jax.ShapeDtypeStruct((pairs, PAIR, total), jnp.float32),
            jax.ShapeDtypeStruct((pairs, 2, total), jnp.float32),
        ],
        scratch_shapes=[pltpu.VMEM((PAIR, total), jnp.bfloat16)],
    )(bias, projected, projected, projected)


def attention_backward(projected, mixed, grad_mixed, logs, bias, first, block=512, chunk=256):
    total = projected.shape[0]
    every = projected.shape[1] // (3 * PAIR)
    pairs = mixed.shape[0]
    block = min(block, total)
    out = jax.ShapeDtypeStruct((total, pairs * PAIR), jnp.bfloat16)
    return pl.pallas_call(
        functools.partial(attention_backward_kernel, chunk=min(chunk, total)),
        name="attention_backward",
        cost_estimate=cost_of(total, pairs, 5),
        grid=(pairs, total // block),
        in_specs=[
            pl.BlockSpec((total, 1), lambda p, i: (0, 0)),
            pl.BlockSpec((block, PAIR), lambda p, i: (i, first + p)),
            pl.BlockSpec((total, PAIR), lambda p, i: (0, every + first + p)),
            pl.BlockSpec((total, PAIR), lambda p, i: (0, 2 * every + first + p)),
            pl.BlockSpec((1, PAIR, block), lambda p, i: (p, 0, i)),
            pl.BlockSpec((block, PAIR), lambda p, i: (i, first + p)),
            pl.BlockSpec((1, 2, block), lambda p, i: (p, 0, i)),
        ],
        out_specs=[
            pl.BlockSpec((block, PAIR), lambda p, i: (i, p)),
            pl.BlockSpec((total, PAIR), lambda p, i: (0, p)),
            pl.BlockSpec((total, PAIR), lambda p, i: (0, p)),
        ],
        out_shape=[out, out, out],
        scratch_shapes=[
            pltpu.VMEM((PAIR, total), jnp.bfloat16),
            pltpu.VMEM((total, PAIR), jnp.float32),
            pltpu.VMEM((total, PAIR), jnp.float32),
        ],
    )(bias, projected, projected, projected, mixed, grad_mixed, logs)


epsilon = 1e-05

CORE_SWAP = ((0, 1), (1, 0), (2, 3), (3, 2))
CHIP_SWAP = ((0, 2), (2, 0), (1, 3), (3, 1))
LOW = jnp.bfloat16
F32 = jnp.float32


def swap_core(values):
    return lax.ppermute(values, "seq", CORE_SWAP)


def swap_chip(values):
    return lax.ppermute(values, "seq", CHIP_SWAP)


def swap_bit(values, size, bit):
    return lax.ppermute(values, "dp", [(i, i ^ bit) for i in range(size)])


def bits_of(size):
    return [1 << b for b in range(size.bit_length() - 1)]


def gather_step(held, size, bit):
    upper = (lax.axis_index("dp") & bit) != 0
    got = swap_bit(held, size, bit)
    first = jnp.where(upper, got, held)
    second = jnp.where(upper, held, got)
    return jnp.stack([first, second], axis=1).reshape((-1,) + held.shape[1:])


def gather_dp(values, size):
    held = values[None]
    for bit in bits_of(size):
        upper = (lax.axis_index("dp") & bit) != 0
        got = swap_bit(held, size, bit)
        held = jnp.concatenate([jnp.where(upper, got, held), jnp.where(upper, held, got)], axis=0)
    return held


def scatter_step(held, size, bit, wire):
    upper = (lax.axis_index("dp") & bit) != 0
    halves = held.reshape((held.shape[0] // 2, 2) + held.shape[1:])
    send = jnp.where(upper, halves[:, 0], halves[:, 1]).astype(wire)
    keep = jnp.where(upper, halves[:, 1], halves[:, 0])
    got = swap_bit(send, size, bit)
    return keep, got


def scatter_dp(values, size, wire, skip=0):
    held = values
    for bit in bits_of(size)[skip:]:
        keep, got = scatter_step(held, size, bit, wire)
        held = keep + got.astype(F32)
    return held[0]


def row_major(values):
    return with_layout_constraint(values, Layout(tuple(range(values.ndim))))


def sinusoid(steps_given, width):
    half = width // 2
    freqs = jnp.exp(-math.log(10000.0) * jnp.arange(half, dtype=F32) / half)
    angles = steps_given.astype(F32)[..., None] * freqs
    return jnp.concatenate([jnp.sin(angles), jnp.cos(angles)], axis=-1)


def norm_parts(values):
    center = values - jnp.mean(values, axis=-1, keepdims=True)
    rate = lax.rsqrt(jnp.mean(center * center, axis=-1, keepdims=True) + epsilon)
    return center * rate, rate


def norm_pull(grad, xhat, rate, gain):
    c = grad * gain
    return rate * (
        c - jnp.mean(c, axis=-1, keepdims=True) - xhat * jnp.mean(c * xhat, axis=-1, keepdims=True)
    )


def gelu_both(values):
    cdf = 0.5 * (1.0 + lax.erf(values * math.sqrt(0.5)))
    slope = cdf + values * (jnp.exp(-0.5 * values * values) * (1.0 / math.sqrt(2.0 * math.pi)))
    return (values * cdf).astype(LOW), slope.astype(LOW)


def rows_dot(left, right):
    return dot32(left, right, (((0,), (0,)), ((), ())))


def column_sums(values):
    return rows_dot(jnp.ones((values.shape[0], 8), LOW), values)[0]


def take_half(values, which, axis):
    size = values.shape[axis] // 2
    return lax.dynamic_slice_in_dim(values, which * size, size, axis)


def layer(
    tokens, timesteps, lengths, time_weight, attn_gain, attn_shift, qkv_weight, out_weight,
    out_bias, mlp_gain, mlp_shift, up_weight, up_bias, down_weight, down_bias, cotangent, *, size
):
    local = tokens.shape[1]
    width = tokens.shape[2]
    half = width // 2
    wide = up_weight.shape[1]
    shard = time_weight.shape[0]
    deep = down_weight.shape[0]
    spot = lax.axis_index("seq")
    row = lax.axis_index("dp")
    chip = spot // 2
    core = spot % 2
    on_one = core == 1
    on_chip_one = chip == 1

    def natural(own, other, axis):
        return jnp.where(
            on_one,
            jnp.concatenate([other, own], axis=axis),
            jnp.concatenate([own, other], axis=axis),
        )

    pieces = [qkv_weight[:, k * half : (k + 1) * half] for k in range(6)]
    qkv_shard = jnp.where(
        on_one, jnp.concatenate(pieces[1::2], axis=1), jnp.concatenate(pieces[0::2], axis=1)
    ).astype(LOW)
    vectors = jnp.concatenate(
        [attn_gain, attn_shift, out_bias, mlp_gain, mlp_shift, down_bias, up_bias]
    ).astype(LOW).astype(F32)
    vectors = jnp.concatenate([timesteps.astype(F32), vectors])[None]
    qkv_shard, vectors, tokens, time_weight, up_weight, down_weight, out_weight = (
        lax.optimization_barrier(
            (qkv_shard, vectors, tokens, time_weight, up_weight, down_weight, out_weight)
        )
    )

    def column_half(values, which):
        half_deep = deep // 2
        return jnp.concatenate(
            [values[:, d * deep + which * half_deep :][:, :half_deep] for d in range(size)], axis=1
        )

    def own_halves(up_weight, down_weight, out_weight):
        up_shard = jnp.where(on_one, column_half(up_weight, 1), column_half(up_weight, 0))
        out_shard = jnp.where(on_one, out_weight[:, half:], out_weight[:, :half])
        return jnp.concatenate(
            [
                up_shard[:, :width],
                up_shard[:, width:],
                take_half(down_weight, core, 0),
                jnp.concatenate([out_shard[: shard // 2], out_shard[shard // 2 :]], axis=1),
            ],
            axis=0,
        ).astype(LOW)

    held = qkv_shard[None]
    for bit in reversed(bits_of(size)):
        if bit == 1:
            held, packed = lax.optimization_barrier(
                (held, own_halves(up_weight, down_weight, out_weight))
            )
        held = gather_step(held, size, bit)
    qkv_own = held.reshape(width, 3 * half)
    own_pack = lax.all_gather(packed, "dp", axis=0, tiled=False)

    def unpack(pack):
        a = pack[:, :shard].reshape(width, width)
        b = pack[:, shard : 2 * shard].reshape(width, width)
        down = pack[:, 2 * shard : 2 * shard + deep // 2].reshape(wide // 2, width)
        return jnp.concatenate([a, b], axis=1), down

    def unpack_out(last):
        return jnp.concatenate([last[:, :, :half], last[:, :, half:]], axis=1).reshape(width, half)

    mine = lax.dynamic_index_in_dim(tokens, chip, 0, False)
    there = lax.dynamic_index_in_dim(tokens, 1 - chip, 0, False)
    source = jnp.concatenate([mine, swap_chip(there)], axis=0)
    small = gather_dp(vectors, size)[:, 0]
    steps = small[:, :2]
    gain_a, shift_a, bias_out, gain_m, shift_m, bias_down = [
        small[:, 2 + k * shard : 2 + (k + 1) * shard].reshape(width) for k in range(6)
    ]
    bias_up = small[:, 2 + 6 * shard :].reshape(size, 2, deep // 2)
    embedded = sinusoid(steps, width).astype(LOW)
    embedded = jnp.where(chip == 1, embedded[:, ::-1], embedded)
    own_rows = lax.dynamic_slice_in_dim(embedded, row * shard, shard, 2)
    time_parts = jnp.dot(own_rows[:, 0], time_weight.astype(LOW), preferred_element_type=F32)
    time_shift = scatter_dp(time_parts[:, None], size, F32)

    length = lax.dynamic_index_in_dim(lengths, chip, 0, False)
    places = jnp.arange(local, dtype=jnp.int32)

    def positions(which):
        return jnp.concatenate(
            [(2 * chip + which) * local + places, (2 * (1 - chip) + which) * local + places]
        )

    own_places = positions(core)
    valid = (own_places < length)[:, None]
    bias = jnp.where(
        jnp.concatenate([own_places, positions(1 - core)]) < length, 0.0, -1e30
    ).astype(F32)[:, None]

    hidden = row_major(row_major(source) + time_shift)
    xhat_a, rate_a = norm_parts(hidden)
    normed_own = (xhat_a * gain_a + shift_a).astype(LOW)
    normed_all = jnp.concatenate([normed_own, swap_core(normed_own)], axis=0)
    projected = jnp.dot(normed_all, qkv_own, preferred_element_type=F32).astype(LOW)
    projected, cotangent = lax.optimization_barrier((projected, cotangent))
    count = hidden.shape[0]
    lead = half // PAIR - 1
    mixed_one, wide_one, logs_one = attention_forward(projected, bias, 0, lead)
    mixed_one, own_pack, projected_late = lax.optimization_barrier((mixed_one, own_pack, projected))
    rest = 2 * shard + deep // 2
    other_out = swap_core(own_pack[:, rest:])
    other_pack = swap_core(own_pack)
    sent_one = swap_core(mixed_one[count:])
    mixed_two, wide_two, logs_two = attention_forward(projected_late, bias, lead, 1)
    attended = natural(
        jnp.concatenate([mixed_one[:count], mixed_two[:count]], axis=1),
        jnp.concatenate([sent_one, swap_core(mixed_two[count:])], axis=1),
        1,
    )

    cot_mine = lax.dynamic_index_in_dim(cotangent, chip, 0, False)
    cot_send = lax.dynamic_index_in_dim(cotangent, 1 - chip, 0, False)
    cot = jnp.concatenate([cot_mine, swap_chip(cot_send)], axis=0)
    cot = row_major(cot)
    out_full = natural(unpack_out(own_pack[:, rest:]), unpack_out(other_out), 1)
    up_a, down_a = unpack(own_pack)
    up_b, down_b = unpack(other_pack)
    bias_up_a = lax.dynamic_index_in_dim(bias_up, core, 1, False).reshape(wide // 2)
    bias_up_b = lax.dynamic_index_in_dim(bias_up, 1 - core, 1, False).reshape(wide // 2)

    middle = hidden + jnp.dot(attended, out_full, preferred_element_type=F32) + bias_out
    middle = row_major(middle)
    xhat_m, rate_m = norm_parts(middle)
    normed_two = (xhat_m * gain_m + shift_m).astype(LOW)
    act_a, slope_a = gelu_both(jnp.dot(normed_two, up_a, preferred_element_type=F32) + bias_up_a)
    act_b, slope_b = gelu_both(jnp.dot(normed_two, up_b, preferred_element_type=F32) + bias_up_b)
    branch = (
        jnp.dot(act_a, down_a, preferred_element_type=F32)
        + jnp.dot(act_b, down_b, preferred_element_type=F32)
        + bias_down
    )
    result = row_major(jnp.where(valid, middle + branch, 0.0))
    result_got = swap_chip(result[local:])

    grad_out = jnp.where(valid, cot, 0.0)
    grad_low = grad_out.astype(LOW)
    pre_a = (dot32(grad_low, down_a, NT) * slope_a.astype(F32)).astype(LOW)
    pre_b = (dot32(grad_low, down_b, NT) * slope_b.astype(F32)).astype(LOW)
    pre_a, pre_b = lax.optimization_barrier((pre_a, pre_b))
    grad_normed_two = row_major(dot32(pre_a, up_a, NT) + dot32(pre_b, up_b, NT))
    grad_middle = row_major(grad_out + norm_pull(grad_normed_two, xhat_m, rate_m, gain_m))
    grad_branch = grad_middle.astype(LOW)
    grad_attended = dot32(grad_branch, out_full, NT).astype(LOW)
    low_half, high_half = grad_attended[:, :half], grad_attended[:, half:]
    heads_own = jnp.where(on_one, high_half, low_half)
    heads_other = swap_core(jnp.where(on_one, low_half, high_half))
    grad_heads = jnp.concatenate([heads_own, heads_other], axis=0)

    def pack_grads(up, down, out):
        parts = [
            up[:, :width].reshape(size, shard, width),
            up[:, width:].reshape(size, shard, width),
            down.reshape(size, deep // 2, width),
        ]
        last = out.reshape(size, shard, half)
        parts.append(jnp.concatenate([last[:, : shard // 2], last[:, shard // 2 :]], axis=2))
        return jnp.concatenate([part.astype(LOW) for part in parts], axis=1)

    out_grad = rows_dot(attended, grad_branch)
    out_low, out_high = out_grad[:, :half], out_grad[:, half:]
    grads_a = pack_grads(
        rows_dot(normed_two, pre_a), rows_dot(act_a, grad_low), jnp.where(on_one, out_high, out_low)
    )
    grads_b = pack_grads(
        rows_dot(normed_two, pre_b), rows_dot(act_b, grad_low), jnp.where(on_one, out_low, out_high)
    )
    summed = (grads_a.astype(F32) + swap_core(grads_b).astype(F32)).astype(LOW)
    grad_heads, summed = lax.optimization_barrier((grad_heads, summed))
    shards = lax.psum_scatter(summed, "dp", scatter_dimension=0, tiled=False)
    cut = lead * PAIR
    grad_a = jnp.concatenate(
        attention_backward(projected, wide_one, grad_heads, logs_one, bias, 0), axis=1
    )
    qkv_a = rows_dot(normed_all, grad_a).reshape(size, 2, shard // 2, 3 * cut)
    qkv_keep = jnp.where(on_chip_one, qkv_a[:, 1], qkv_a[:, 0])
    qkv_send = jnp.where(on_chip_one, qkv_a[:, 0], qkv_a[:, 1]).astype(LOW)
    qkv_got = swap_chip(qkv_send)
    grad_b = jnp.concatenate(
        attention_backward(projected, wide_two, grad_heads, logs_two, bias, lead), axis=1
    )
    columns = [qkv_own[:, k * half : (k + 1) * half] for k in range(3)]
    weight_a = jnp.concatenate([part[:, :cut] for part in columns], axis=1)
    weight_b = jnp.concatenate([part[:, cut:] for part in columns], axis=1)
    part_other = dot32(grad_a[count:], weight_a, NT) + dot32(grad_b[count:], weight_b, NT)
    part_other = swap_core(part_other.astype(LOW))
    qkv_b = rows_dot(normed_all, grad_b).reshape(size, shard, 3 * (half - cut))
    qkv_a, qkv_b, grad_a, grad_b, pre_a, pre_b, grad_branch, grad_low, grad_normed_two = (
        lax.optimization_barrier(
            (
                qkv_keep + qkv_got.astype(F32),
                qkv_b, grad_a, grad_b, pre_a, pre_b, grad_branch, grad_low, grad_normed_two,
            )
        )
    )
    keep_b, got_b = scatter_step(qkv_b, size, 1, LOW)
    keep_a, got_a = scatter_step(qkv_a, size, 1, LOW)

    part_own = dot32(grad_a[:count], weight_a, NT) + dot32(grad_b[:count], weight_b, NT)
    grad_normed_one = row_major(part_own + part_other.astype(F32))
    tokens_grad = row_major(
        grad_middle + norm_pull(grad_normed_one, xhat_a, rate_a, gain_a)
    )

    sum_bias_up = natural(
        column_sums(pre_a).reshape(size, 1, deep // 2),
        column_sums(pre_b).reshape(size, 1, deep // 2),
        1,
    ).reshape(size, deep)
    vector_sums = jnp.concatenate(
        [
            jnp.sum(grad_normed_one * xhat_a, axis=0).reshape(size, shard),
            jnp.sum(grad_normed_one, axis=0).reshape(size, shard),
            column_sums(grad_branch).reshape(size, shard),
            jnp.sum(grad_normed_two * xhat_m, axis=0).reshape(size, shard),
            jnp.sum(grad_normed_two, axis=0).reshape(size, shard),
            column_sums(grad_low).reshape(size, shard),
            sum_bias_up,
        ],
        axis=1,
    )
    token_sum = jnp.sum(tokens_grad, axis=0, keepdims=True)
    sums = jnp.concatenate([vector_sums.reshape(1, -1), token_sum], axis=1)
    sums, got_a, got_b = lax.optimization_barrier((sums, got_a, got_b))
    sums = sums + swap_core(sums)
    sums_there = swap_chip(sums)
    sums_there, result_got, result = lax.optimization_barrier((sums_there, result_got, result))
    tokens_got = swap_chip(tokens_grad[local:].astype(LOW)).astype(F32)
    vector_sums = (sums + sums_there)[:, : vector_sums.size].reshape(vector_sums.shape)
    vector_mine = scatter_dp(vector_sums[:, None], size, F32)[0]
    vector_out = [vector_mine[k * shard : (k + 1) * shard] for k in range(6)]
    both = jnp.concatenate([sums, sums_there], axis=0)[:, -width:]
    gathered = gather_dp(both, size)
    sums_own = gathered[:, 0]
    sums_other = gathered[:, 1]
    qkv_a = scatter_dp(keep_a + got_a.astype(F32), size, LOW, 1)
    qkv_b = scatter_dp(keep_b + got_b.astype(F32), size, LOW, 1)
    qkv_more = swap_chip(qkv_a)
    qkv_a = jnp.where(
        on_chip_one,
        jnp.concatenate([qkv_more, qkv_a], axis=0),
        jnp.concatenate([qkv_a, qkv_more], axis=0),
    )
    qkv_b = qkv_b + swap_chip(qkv_b.astype(LOW)).astype(F32)
    qkv_mine = jnp.concatenate(
        [
            piece
            for k in range(3)
            for piece in (
                qkv_a[:, k * cut : (k + 1) * cut],
                qkv_b[:, k * (half - cut) : (k + 1) * (half - cut)],
            )
        ],
        axis=1,
    )
    qkv_other = swap_core(qkv_mine)
    qkv_out = jnp.concatenate(
        [
            natural(
                qkv_mine[:, k * half : (k + 1) * half], qkv_other[:, k * half : (k + 1) * half], 1
            )
            for k in range(3)
        ],
        axis=1,
    )

    exact = dict(precision=lax.Precision.HIGHEST, preferred_element_type=F32)
    contract = (((0,), (0,)), ((), ()))
    time_grad = lax.dot_general(
        own_rows[:, 0].astype(F32), sums_own, contract, **exact
    ) + lax.dot_general(own_rows[:, 1].astype(F32), sums_other, contract, **exact)

    shards = shards.astype(F32)
    shards = shards + swap_chip(shards.astype(LOW)).astype(F32)
    shards_other = swap_core(shards.astype(LOW)).astype(F32)

    def unpack_grads(pack):
        up = jnp.concatenate([pack[:shard], pack[shard : 2 * shard]], axis=1)
        down = pack[2 * shard : 2 * shard + deep // 2]
        last = pack[2 * shard + deep // 2 :]
        return up, down, jnp.concatenate([last[:, :half], last[:, half:]], axis=0)

    up_ga, down_ga, out_ga = unpack_grads(shards)
    up_gb, down_gb, out_gb = unpack_grads(shards_other)
    up_low = jnp.where(on_one, up_gb, up_ga)
    up_high = jnp.where(on_one, up_ga, up_gb)
    up_out = jnp.concatenate(
        [
            side[:, d * (deep // 2) : (d + 1) * (deep // 2)]
            for d in range(size)
            for side in (up_low, up_high)
        ],
        axis=1,
    )

    def hand_back(kept, got):
        return row_major(
            jnp.where(on_chip_one, jnp.stack([got, kept]), jnp.stack([kept, got]))
        )

    return (
        hand_back(result[:local], result_got),
        hand_back(tokens_grad[:local], tokens_got),
        time_grad,
        vector_out[0],
        vector_out[1],
        qkv_out,
        natural(out_ga, out_gb, 1),
        vector_out[2],
        vector_out[3],
        vector_out[4],
        up_out,
        vector_mine[6 * shard :],
        natural(down_ga, down_gb, 0),
        vector_out[5],
    )


def solution(mesh):
    batch = P("dp", "seq", None)
    flat = P("dp")
    grid = P("dp", None)
    in_specs = (
        batch, flat, flat, grid, flat, flat, grid, grid, flat, flat, flat, grid, flat, grid, flat,
        batch,
    )
    out_specs = (
        batch, batch, grid, flat, flat, grid, grid, flat, flat, flat, grid, flat, grid, flat,
    )
    body = functools.partial(layer, size=mesh.shape["dp"])
    return jax.shard_map(
        body, mesh=mesh, in_specs=in_specs, out_specs=out_specs, check_vma=False
    )
```
